512 devices in a mesh: teacher: 16 (over z_hi, x, core), vocab: 32 (over z_lo, y).
Axes of the slice: x: 4, y: 4, z: 16 (z_hi: 2, z_lo: 8; z = z_hi * 8 + z_lo), core: 2. Of those that a mesh axis runs over, the one named last changes fastest.
Arguments:
- teacher_hidden: bfloat16 [16, 128, 2048], P('teacher', 'vocab'), may hold values from -32 to 32
- teacher_head: bfloat16 [2048, 65536], P('teacher', 'vocab'), may hold values from -1 to 1
- student_hidden: bfloat16 [128, 2048], P(None, 'teacher'), may hold values from -32 to 32
- student_head: bfloat16 [2048, 65536], P('teacher', 'vocab'), may hold values from -1 to 1
- labels: int32 [128], P('teacher'), may hold values from 0 to 65535
Outputs:
- ce_matrix: float32 [128, 16, 16], P('teacher')
- agreement: float32 [128, 16], P('teacher')
- student_grad: float32 [2048, 65536], P('teacher', 'vocab')
The draws below stay inside these ranges and needn't reach their ends.
All inputs are finite; a program needn't handle non-finite values.
Results may differ from the reference program's by a relative error of at most 0.0065.
Values may be sent and summed in bfloat16 or wider, within the bound.
A program may use at most 64 MiB of HBM per device.

```python
import math
import jax
import jax.numpy as jnp
from jax import lax

D = 2048
TOKENS = 128
TEACHERS = 16
VOCAB = 65536


def head_columns(key, stream, chosen_cols):
    head_key = jax.random.fold_in(key, stream)

    def one_column(column):
        return jax.random.normal(jax.random.fold_in(head_key, column), (D,), jnp.float32)
    values = jax.vmap(one_column)(chosen_cols)
    return jnp.clip(values * (3.0 / math.sqrt(D)), -1.0, 1.0)


def draw_head(key, stream):
    return head_columns(key, stream, jnp.arange(VOCAB, dtype=jnp.int32)).T.astype(jnp.bfloat16)


def strength_levels():
    levels = jnp.array([30.0, 45.0, 60.0], jnp.float32)
    return levels


def peak_rows(key, stream, first_cols, second_cols, first_logit, second_logit):
    first_vecs = head_columns(key, stream, first_cols)
    second_vecs = head_columns(key, stream, second_cols)
    first_square = jnp.sum(first_vecs * first_vecs, axis=1, keepdims=True)
    cross_dot = jnp.sum(first_vecs * second_vecs, axis=1, keepdims=True)
    along_ratio = cross_dot / first_square
    normal_part = second_vecs - along_ratio * first_vecs
    normal_square = jnp.sum(normal_part * normal_part, axis=1, keepdims=True)
    along_second = second_logit[:, None] - along_ratio * first_logit[:, None]
    peaked = first_logit[:, None] * first_vecs / first_square + along_second * normal_part / normal_square
    return jnp.clip(peaked, -32.0, 32.0)


def column_pair(key, stream, count):
    first_cols = jax.random.randint(jax.random.fold_in(key, stream), (count,), 0, VOCAB)
    offsets = jax.random.randint(jax.random.fold_in(key, stream + 1), (count,), 1, VOCAB)
    return (first_cols, (first_cols + offsets) % VOCAB)


def scaled_rows(key, plain_rows):
    result = plain_rows
    return result


def draw_teacher_head(key, part):
    return draw_head(key, 10)


def draw_student_head(key, part):
    return draw_head(key, 20)


def draw_teacher_hidden(key, part):
    plain_rows = jnp.clip(jax.random.normal(jax.random.fold_in(key, 11), (TEACHERS, TOKENS, D), jnp.float32), -6.0, 6.0)
    plain_rows = scaled_rows(key, plain_rows)
    marked_count = TOKENS // 4
    marked_ids = 4 * jnp.arange(marked_count, dtype=jnp.int32) + 1
    first_cols, second_cols = column_pair(key, 14, marked_count)
    level_pick = jax.random.randint(jax.random.fold_in(key, 16), (TEACHERS, marked_count), 0, 3)
    leading = jax.random.randint(jax.random.fold_in(key, 17), (TEACHERS, marked_count), 0, 2).astype(jnp.float32)
    top_logit = strength_levels()[level_pick]
    first_logit = (top_logit - 2.0 * (1.0 - leading)).reshape(-1)
    second_logit = (top_logit - 2.0 * leading).reshape(-1)
    first_all = jnp.broadcast_to(first_cols[None, :], (TEACHERS, marked_count)).reshape(-1)
    second_all = jnp.broadcast_to(second_cols[None, :], (TEACHERS, marked_count)).reshape(-1)
    peaked = peak_rows(key, 10, first_all, second_all, first_logit, second_logit).reshape(TEACHERS, marked_count, D)
    result = plain_rows.at[:, marked_ids, :].set(peaked)
    return result.astype(jnp.bfloat16)


def draw_student_hidden(key, part):
    shared = jnp.clip(jax.random.normal(jax.random.fold_in(key, 21), (1, D), jnp.float32), -4.0, 4.0)
    noise_rows = jnp.clip(jax.random.normal(jax.random.fold_in(key, 22), (TOKENS, D), jnp.float32), -4.0, 4.0)
    plain_rows = 0.2 * (shared + noise_rows)
    plain_rows = scaled_rows(key, plain_rows)
    first_cols, second_cols = column_pair(key, 24, TOKENS)
    level_pick = jax.random.randint(jax.random.fold_in(key, 26), (TOKENS,), 0, 3)
    top_logit = strength_levels()[level_pick]
    peaked = peak_rows(key, 20, first_cols, second_cols, top_logit, top_logit - 2.0)
    marked = jnp.arange(TOKENS, dtype=jnp.int32) % 16 == 6
    result = jnp.where(marked[:, None], peaked, plain_rows)
    return result.astype(jnp.bfloat16)


def set_ends(values, rng, least, top_value):
    extent = values.shape
    place = [jax.random.randint(jax.random.fold_in(rng, axis), (), 0, extent[axis]) for axis in range(len(extent))]
    values = values.at[tuple(place)].set(least)
    longest = extent.index(max(extent))
    place[longest] = (place[longest] + 1) % extent[longest]
    return values.at[tuple(place)].set(top_value)


def setup_inputs(seed: int = 0) -> dict:
    key_of = jax.random.split(jax.random.key(seed), 6)
    return {
        "teacher_hidden": draw_teacher_hidden(jax.random.fold_in(key_of[5], 71), 0),
        "teacher_head": draw_teacher_head(jax.random.fold_in(key_of[5], 71), 0),
        "student_hidden": draw_student_hidden(jax.random.fold_in(key_of[5], 71), 0),
        "student_head": draw_student_head(jax.random.fold_in(key_of[5], 71), 0),
        "labels": set_ends(jax.random.randint(key_of[4], (TOKENS,), 0, VOCAB), jax.random.fold_in(key_of[4], 1), 0, VOCAB - 1).astype(jnp.int32),
    }


HARD_SHARE = 0.3


def log_softmax(logits):
    highest = jnp.max(logits, axis=1, keepdims=True)
    summed = jnp.sum(jnp.exp(logits - highest), axis=1, keepdims=True)
    return logits - (highest + jnp.log(summed))


def reference(teacher_hidden, teacher_head, student_hidden, student_head, labels):
    def teacher_rows(hidden):
        logits = jnp.dot(hidden, teacher_head, preferred_element_type=jnp.float32)
        return log_softmax(logits).astype(jnp.bfloat16)

    log_probs = lax.map(teacher_rows, teacher_hidden)
    teacher_prob = jnp.exp(log_probs.astype(jnp.float32)).astype(jnp.bfloat16)
    block_rows = TOKENS // TEACHERS
    columns = jnp.arange(VOCAB, dtype=jnp.int32)

    def block_terms(block_index):
        offset = (block_index * block_rows).astype(jnp.int32)
        prob_block = lax.dynamic_slice_in_dim(teacher_prob, offset, block_rows, 1).astype(jnp.float32)
        logprob_block = lax.dynamic_slice_in_dim(log_probs, offset, block_rows, 1).astype(jnp.float32)
        cross_block = -jnp.einsum("itv,jtv->tij", prob_block, logprob_block)
        disagree = jnp.mean(cross_block, axis=1)
        inverse = 1.0 / (1.0 + disagree)
        weights = inverse / jnp.sum(inverse, axis=1, keepdims=True)
        soft_mix = jnp.einsum("ti,itv->tv", weights, prob_block)
        label_block = lax.dynamic_slice_in_dim(labels, offset, block_rows, 0)
        onehot = (columns[None, :] == label_block[:, None]).astype(jnp.float32)
        target = (1.0 - HARD_SHARE) * soft_mix + HARD_SHARE * onehot
        hidden_block = lax.dynamic_slice_in_dim(student_hidden, offset, block_rows, 0)
        student_logits = jnp.dot(hidden_block, student_head, preferred_element_type=jnp.float32)
        student_prob = jnp.exp(log_softmax(student_logits))
        residual = (student_prob - target).astype(jnp.bfloat16)
        return cross_block, weights * TEACHERS, residual

    cross_all, agreement, residual = lax.map(block_terms, jnp.arange(TEACHERS, dtype=jnp.int32))
    cross_all = cross_all.reshape(TOKENS, TEACHERS, TEACHERS)
    agreement = agreement.reshape(TOKENS, TEACHERS)
    residual = residual.reshape(TOKENS, VOCAB)
    student_grad = lax.dot_general(student_hidden, residual, (((0,), (0,)), ((), ())), preferred_element_type=jnp.float32)
    return (cross_all, agreement, student_grad)
```

```python
import jax
import jax.numpy as jnp
from jax import lax
from jax.experimental import pallas as pl
from jax.experimental.pallas import tpu as pltpu
from jax.sharding import PartitionSpec as P

HARD_SHARE = 0.3
MESH = pl.DeviceIdType.MESH
F32 = jnp.float32
BF16 = jnp.bfloat16
I32 = jnp.int32


def iota(shape, dim):
    return lax.broadcasted_iota(I32, shape, dim)


def row_token(r):
    return (r >> 3) & 15


def row_teacher(r):
    return (r >> 7) * 8 + (r & 7)


def fold_tokens(values):
    same = row_token(iota((256, 256), 0)) == row_token(iota((256, 256), 1))
    kept = jnp.where(same, values, 0.0).reshape(2, 16, 8, 256)
    return jnp.sum(kept, axis=1).reshape(16, 256)


def own_lane(values):
    same = iota((16, 256), 0) == row_teacher(iota((16, 256), 1))
    return jnp.sum(jnp.where(same, values, 0.0), axis=0, keepdims=True)


def kernel(
    hid_in, head, sh, shead, lab_in,
    grad_out, ce_out, agree_out,
    W, relay, hx, hid, L, Eb, Cb, mbuf, sbuf,
    S, Sc, A, Sx, T, Sz, SL, lab, yb, xb, rb, gb, R,
    s_z, s_rf, s_xl, s_xf, s_c, s_h1, s_h2, s_h3, s_st, s_y, s_z1, s_z2, s_r,
    r_relay, r_w, r_h1, r_h2, r_sc, r_sx, r_sz, r_lab, r_y, r_z1, r_z2, r_r, l_w,
):
    t = lax.axis_index("teacher")
    v = lax.axis_index("vocab")
    zh, xc = t // 8, t % 8
    x, c = xc // 2, xc % 2
    zl, y = v // 4, v % 4
    z = zh * 8 + zl

    def dev(z_, xc_, y_):
        return {"teacher": (z_ // 8) * 8 + xc_, "vocab": (z_ % 8) * 4 + y_}

    def send(src, dst, ssem, rsem, to):
        pltpu.make_async_remote_copy(
            src_ref=src, dst_ref=dst, send_sem=ssem, recv_sem=rsem, device_id=to, device_id_type=MESH
        ).start()

    def done(ref, sem):
        pltpu.make_async_copy(ref, ref, sem).wait()

    def each(lo, hi, body):
        def step(i, carry):
            body(i)
            return carry
        lax.fori_loop(lo, hi, step, 0)

    z_to = lambda d: dev((z + d) % 16, xc, y)
    x_to = lambda d: dev(z, ((x + d) % 4) * 2 + c, y)
    y_to = lambda d: dev(z, xc, (y + d) % 4)
    xc_to = lambda d: dev(z, (xc + d) % 8, y)
    sibling = dev(z, x * 2 + 1 - c, y)
    partner = z_to(8)

    barrier = pltpu.get_barrier_semaphore()
    each(1, 16, lambda d: pl.semaphore_signal(barrier, inc=1, device_id=z_to(d), device_id_type=MESH))
    each(1, 8, lambda d: pl.semaphore_signal(barrier, inc=1, device_id=xc_to(d), device_id_type=MESH))
    each(1, 4, lambda d: pl.semaphore_signal(barrier, inc=1, device_id=y_to(d), device_id_type=MESH))
    pl.semaphore_wait(barrier, 25)

    mine = pl.ds(pl.multiple_of(zh * 1024, 1024), 1024)
    other = pl.ds(pl.multiple_of((1 - zh) * 1024, 1024), 1024)
    piece = lambda zh_, x_, c_, half: ((zh_ * 8 + x_ * 2 + c_) * 2) + half
    w_at = lambda p: W.at[pl.ds(pl.multiple_of(p * 64, 64), 64), :]

    for half, d in ((0, 4), (1, 12)):
        send(head.at[pl.ds(half * 64, 64), other], relay.at[half], s_z.at[half], r_relay.at[half], z_to(d))
    spread = (z % 4) * 2 + y // 2
    is_spread = xc == spread
    to_spread = dev(z, spread, y)

    @pl.when(is_spread)
    def _():
        pltpu.make_async_copy(hid_in, hx.at[xc], r_h1.at[xc]).start()

    @pl.when(jnp.logical_not(is_spread))
    def _():
        send(hid_in, hx.at[xc], s_h1.at[0], r_h1.at[xc], to_spread)

    for half in range(2):
        p = piece(zh, x, c, half)
        src = head.at[pl.ds(half * 64, 64), mine]
        send(src, w_at(p), s_xl.at[half * 2], r_w.at[p], x_to(1))
        send(src, w_at(p), s_xl.at[half * 2 + 1], r_w.at[p], x_to(3))
        send(src, w_at(p), s_c.at[p], r_w.at[p], sibling)
        pltpu.make_async_copy(src, w_at(p), l_w.at[half]).start()
    lab[pl.ds(zh, 1)] = lab_in[...][None]
    send(lab.at[zh], lab.at[zh], s_st.at[5], r_lab.at[0], partner)

    for k in range(4):
        cols = pl.ds(k * 512, 512)
        S[:, :, :, :, cols] = jnp.dot(sh[...], shead[:, cols], preferred_element_type=F32).reshape(2, 4, 2, 8, 512)
    send(S.at[:, :, 1 - c], Sc, s_st.at[0], r_sc.at[0], sibling)

    k_spread = (z // 8) * 4 + ((z % 8) // 4) * 2 + y % 2

    def hid_at(k):
        return hid.at[pl.ds(pl.multiple_of(k * 32, 32), 32), :]

    @pl.when(is_spread)
    def _():
        each(0, 8, lambda i: done(hx.at[i], r_h1.at[i]))
        r, s = iota((128, 128), 0), iota((128, 128), 1)
        perm = ((s >> 4) == (r & 7)) & (((s >> 2) & 3) == (r >> 5)) & ((s & 3) == ((r >> 3) & 3))
        rows = jnp.dot(
            jnp.where(perm, 1.0, 0.0).astype(BF16), hx[...].reshape(128, 512), preferred_element_type=F32
        ).astype(BF16)
        for q in range(4):
            hid[pl.ds(pl.multiple_of(k_spread * 32, 32), 32), pl.ds(q * 512, 512)] = rows[q * 32:(q + 1) * 32]
        each(1, 16, lambda d: send(
            hid_at(k_spread), hid_at(k_spread), s_h2.at[d], r_h2.at[k_spread], z_to(d)))

    for half, d in ((0, 4), (1, 12)):
        zd = (z + d) % 16
        p = piece(1 - zd // 8, x, c, half)
        done(relay.at[half], r_relay.at[half])
        send(relay.at[half], w_at(p), s_rf.at[half], r_w.at[p], dev(zd, xc, y))

    def ring(zg):
        left, right, far = (x + 3) % 4, (x + 1) % 4, (x + 2) % 4
        for half in range(2):
            near, turn = (left, 1) if half == 0 else (right, 3)
            p = piece(zg, near, c, half)
            done(w_at(p), r_w.at[p])
            send(w_at(p), w_at(p), s_xf.at[zg * 2 + half], r_w.at[p], x_to(turn))
            send(w_at(p), w_at(p), s_c.at[p], r_w.at[p], sibling)
        for half in range(2):
            near = right if half == 0 else left
            p = piece(zg, near, c, half)
            done(w_at(p), r_w.at[p])
            send(w_at(p), w_at(p), s_c.at[p], r_w.at[p], sibling)
        for half in range(2):
            p = piece(zg, far, c, half)
            done(w_at(p), r_w.at[p])
            send(w_at(p), w_at(p), s_c.at[p], r_w.at[p], sibling)

    @pl.when(y // 2 == c)
    def _():
        def go(k4):
            k = k4 * 2 + y % 2

            @pl.when(jnp.logical_not(jnp.logical_and(is_spread, k == k_spread)))
            def _():
                done(hid_at(k), r_h2.at[k])

            each(1, 4, lambda d: send(hid_at(k), hid_at(k), s_h3.at[k4 * 3 + d - 1], r_h2.at[k], y_to(d)))
        each(0, 4, go)

    done(Sc, r_sc.at[0])
    for h in range(2):
        for x_ in range(4):
            A[x_, h] = S[h, x_, c] + Sc[h, x_]
    each(1, 4, lambda d: send(A.at[(x + d) % 4], Sx.at[x], s_st.at[d], r_sx.at[x], x_to(d)))

    ring(zh)

    each(1, 4, lambda d: done(Sx.at[(x + d) % 4], r_sx.at[(x + d) % 4]))
    total = A[x] + Sx[(x + 1) % 4] + Sx[(x + 2) % 4] + Sx[(x + 3) % 4]
    T[0] = total[:, :, :1024]
    T[1] = total[:, :, 1024:]
    send(T.at[1 - zh], Sz, s_st.at[4], r_sz.at[0], partner)

    for half in range(2):
        p = piece(1 - zh, x, c, half)
        done(w_at(p), r_w.at[p])
        send(w_at(p), w_at(p), s_xl.at[4 + half * 2], r_w.at[p], x_to(1))
        send(w_at(p), w_at(p), s_xl.at[5 + half * 2], r_w.at[p], x_to(3))
        send(w_at(p), w_at(p), s_c.at[p], r_w.at[p], sibling)
    ring(1 - zh)

    def last_hidden(k):
        @pl.when(jnp.logical_not(jnp.logical_and(y // 2 == c, y % 2 == k % 2)))
        def _():
            done(hid_at(k), r_h2.at[k])
    each(0, 8, last_hidden)

    done(Sz, r_sz.at[0])
    student = (T[zh] + Sz[...]).reshape(16, 1024)
    SL[...] = student
    s_top = jnp.max(student, axis=1, keepdims=True)
    s_sum = jnp.sum(jnp.exp(student - s_top), axis=1, keepdims=True)
    mine_tok = row_token(iota((16, 128), 1)) == iota((16, 128), 0)
    s_top = jnp.sum(jnp.where(mine_tok, s_top, 0.0), axis=0, keepdims=True)
    s_sum = jnp.sum(jnp.where(mine_tok, s_sum, 0.0), axis=0, keepdims=True)

    def from_sibling(i):
        p = (i // 2) * 4 + (1 - c) * 2 + i % 2
        done(w_at(p), r_w.at[p])
    each(0, 16, from_sibling)
    for half in range(2):
        p = piece(zh, x, c, half)
        pltpu.make_async_copy(head.at[pl.ds(half * 64, 64), mine], w_at(p), l_w.at[half]).wait()

    def scores(n):
        cols = pl.ds(pl.multiple_of(n * 256, 256), 256)
        L[:, cols] = jnp.dot(hid[...], W[:, cols], preferred_element_type=F32)
    each(0, 4, scores)

    def local_stats(n):
        rows = pl.ds(pl.multiple_of(n * 32, 32), 32)
        logits = L[rows, :]
        top = jnp.max(logits, axis=1, keepdims=True)
        low = logits - top
        e = jnp.exp(low)
        Eb[rows, :] = e.astype(BF16)
        Cb[rows, :] = low.astype(BF16)
        mbuf[rows, :] = jnp.broadcast_to(top, (32, 128))
        sbuf[rows, :] = jnp.broadcast_to(jnp.sum(e, axis=1, keepdims=True), (32, 128))
    each(0, 8, local_stats)

    cross = fold_tokens(lax.dot_general(
        Eb[...], Cb[...], (((1,), (1,)), ((), ())), preferred_element_type=F32))
    tops = mbuf[...]
    tops = fold_tokens(jnp.concatenate([tops, tops], axis=1))
    sums = sbuf[...]
    sums = fold_tokens(jnp.concatenate([sums, sums], axis=1))
    local_top = own_lane(tops)
    cross = cross + sums * local_top
    yb[y, 0:2] = cross.reshape(2, 8, 256)
    yb[y, 2:4] = tops.reshape(2, 8, 256)
    yb[y, 4:6] = sums.reshape(2, 8, 256)
    yb[y, 6] = jnp.broadcast_to(jnp.concatenate([s_top, s_sum], axis=1), (8, 256))
    each(1, 4, lambda d: send(yb.at[y], yb.at[y], s_y.at[d], r_y.at[y], y_to(d)))
    each(1, 4, lambda d: done(yb.at[(y + d) % 4], r_y.at[(y + d) % 4]))
    got = yb[...]
    y_top = jnp.max(got[:, 2:4], axis=0)
    y_scale = jnp.exp(got[:, 2:4] - y_top[None])
    xb[:, 0, :] = jnp.sum(got[:, 0:2] * y_scale, axis=0).reshape(16, 256)
    xb[:, 1, :] = y_top.reshape(16, 256)
    xb[:, 2, :] = jnp.sum(got[:, 4:6] * y_scale, axis=0).reshape(16, 256)
    y_stop = jnp.max(got[:, 6, :, :128], axis=0)
    y_ssum = jnp.sum(got[:, 6, :, 128:] * jnp.exp(got[:, 6, :, :128] - y_stop[None]), axis=0)
    s_row = jnp.concatenate([y_stop, y_ssum], axis=1)
    xb[:, 3, :] = jnp.concatenate([s_row, s_row], axis=0)

    each(1, 16, lambda d: send(xb.at[(z + d) % 16], rb.at[z], s_z1.at[d], r_z1.at[z], z_to(d)))
    rb[pl.ds(z, 1)] = xb[pl.ds(z, 1)]
    each(1, 16, lambda d: done(rb.at[(z + d) % 16], r_z1.at[(z + d) % 16]))
    z_tops = rb[:, 1, :]
    z_top = jnp.max(z_tops, axis=0, keepdims=True)
    z_scale = jnp.exp(z_tops - z_top)
    z_sum = jnp.sum(rb[:, 2, :] * z_scale, axis=0, keepdims=True)
    z_cross = jnp.sum(rb[:, 0, :] * z_scale, axis=0, keepdims=True) / z_sum
    stud = rb[:, 3, :]
    stud_top = jnp.max(stud[:, :128], axis=0, keepdims=True)
    stud_sum = jnp.sum(stud[:, 128:] * jnp.exp(stud[:, :128] - stud_top), axis=0, keepdims=True)
    stud_norm = stud_top + jnp.log(stud_sum)
    gb[pl.ds(z, 1)] = jnp.concatenate([z_cross, z_top + jnp.log(z_sum)], axis=0)[None]
    each(1, 16, lambda d: send(gb.at[z], gb.at[z], s_z2.at[d], r_z2.at[z], z_to(d)))
    each(1, 16, lambda d: done(gb.at[(z + d) % 16], r_z2.at[(z + d) % 16]))
    norm = own_lane(gb[:, 1, :])
    ce = norm - gb[:, 0, :]
    ce_out[...] = ce
    inverse = 1.0 / (1.0 + jnp.sum(ce, axis=0, keepdims=True) / 16.0)
    r, l = iota((256, 256), 0), iota((256, 256), 1)
    by_row = jnp.sum(jnp.where(r == l, inverse, 0.0), axis=1, keepdims=True)
    share = jnp.sum(jnp.where(row_token(r) == row_token(l), by_row, 0.0), axis=0, keepdims=True)
    weights = inverse / share
    agree_out[...] = jnp.broadcast_to(weights * 16.0, (8, 256))
    scale = weights * jnp.exp(local_top - norm)
    spread_w = jnp.where(iota((16, 256), 0) == row_token(iota((16, 256), 1)), scale, 0.0)
    coarse = spread_w.astype(BF16)
    fine = (spread_w - coarse.astype(F32)).astype(BF16)
    soft = jnp.dot(coarse, Eb[...], preferred_element_type=F32) + jnp.dot(fine, Eb[...], preferred_element_type=F32)

    done(lab.at[1 - zh], r_lab.at[0])
    lane = iota((16, 128), 1)
    first = (row_token(lane) == iota((16, 128), 0)) & ((lane & 7) == 0)
    s_norm = jnp.sum(jnp.where(first, stud_norm, 0.0), axis=1, keepdims=True)
    ids = lab[...].reshape(16, 128)
    ids = jnp.concatenate([ids] * 8, axis=1)
    onehot = jnp.where(iota((16, 1024), 1) + (v * 2048 + zh * 1024) == ids, HARD_SHARE, 0.0)
    residual = jnp.exp(SL[...] - s_norm) - ((1.0 - HARD_SHARE) * soft + onehot)
    R[zh, xc] = residual.astype(BF16)

    send(R.at[zh, xc], R.at[zh, xc], s_r.at[0], r_r.at[zh * 8 + xc], partner)

    def spread_r(zg, base):
        each(1, 8, lambda d: send(R.at[zg, xc], R.at[zg, xc], s_r.at[base + d], r_r.at[zg * 8 + xc], xc_to(d)))
    spread_r(zh, 0)
    done(R.at[1 - zh, xc], r_r.at[(1 - zh) * 8 + xc])
    spread_r(1 - zh, 7)
    tokens = sh[...].astype(F32).reshape(2, 8, 8, 128)
    tokens = jnp.swapaxes(tokens, 0, 1).reshape(128, 128).astype(BF16)
    for f in range(2):
        each(1, 8, lambda d: done(R.at[f, (xc + d) % 8], r_r.at[f * 8 + (xc + d) % 8]))
        for k in range(2):
            grad_out[:, pl.ds(f * 1024 + k * 512, 512)] = lax.dot_general(
                tokens, R[f, :, :, pl.ds(k * 512, 512)].reshape(128, 512),
                (((0,), (0,)), ((), ())), preferred_element_type=F32)

    for half in range(2):
        done(relay.at[half], s_z.at[half])
        done(relay.at[half], s_rf.at[half])
    for i in range(8):
        done(w_at(0), s_xl.at[i])
    for i in range(4):
        done(w_at(0), s_xf.at[i])

    def own_core(i):
        p = (i // 2) * 4 + c * 2 + i % 2
        done(w_at(p), s_c.at[p])
    each(0, 16, own_core)

    @pl.when(jnp.logical_not(is_spread))
    def _():
        done(hx.at[0], s_h1.at[0])

    @pl.when(is_spread)
    def _():
        each(1, 16, lambda d: done(hid_at(0), s_h2.at[d]))

    @pl.when(y // 2 == c)
    def _():
        each(0, 12, lambda i: done(hid_at(0), s_h3.at[i]))
    done(Sc, s_st.at[0])
    each(1, 4, lambda d: done(A.at[0], s_st.at[d]))
    done(Sz, s_st.at[4])
    done(lab.at[0], s_st.at[5])
    each(1, 4, lambda d: done(yb.at[0], s_y.at[d]))
    each(1, 16, lambda d: done(rb.at[0], s_z1.at[d]))
    each(1, 16, lambda d: done(gb.at[0], s_z2.at[d]))
    each(0, 15, lambda i: done(R.at[0, 0], s_r.at[i]))


def on_device(teacher_hidden, teacher_head, student_hidden, student_head, labels):
    hid = teacher_hidden[0].reshape(4, 4, 512).transpose(1, 0, 2).reshape(16, 512)
    lab = jnp.broadcast_to(labels[:, None], (8, 128))
    vmem = lambda shape, dtype=F32: pltpu.VMEM(shape, dtype)
    dma = lambda n: pltpu.SemaphoreType.DMA((n,))
    space = pl.BlockSpec(memory_space=pltpu.VMEM)
    grad, ce, agree = pl.pallas_call(
        kernel,
        out_shape=(
            jax.ShapeDtypeStruct((128, 2048), F32),
            jax.ShapeDtypeStruct((16, 256), F32),
            jax.ShapeDtypeStruct((8, 256), F32),
        ),
        in_specs=[space] * 5,
        out_specs=(space,) * 3,
        scratch_shapes=[
            vmem((2048, 1024), BF16), vmem((2, 64, 1024), BF16), vmem((8, 16, 512), BF16), vmem((256, 2048), BF16),
            vmem((256, 1024)), vmem((256, 1024), BF16), vmem((256, 1024), BF16), vmem((256, 128)), vmem((256, 128)),
            vmem((2, 4, 2, 8, 2048)), vmem((2, 4, 8, 2048)), vmem((4, 2, 8, 2048)), vmem((4, 2, 8, 2048)),
            vmem((2, 2, 8, 1024)), vmem((2, 8, 1024)), vmem((16, 1024)), vmem((2, 8, 128), I32),
            vmem((4, 7, 8, 256)), vmem((16, 4, 256)), vmem((16, 4, 256)), vmem((16, 2, 256)),
            vmem((2, 8, 16, 1024), BF16),
            dma(2), dma(2), dma(8), dma(4), dma(32), dma(1), dma(16), dma(12), dma(6), dma(4), dma(16), dma(16), dma(15),
            dma(2), dma(32), dma(8), dma(8), dma(1), dma(4), dma(1), dma(1), dma(4), dma(16), dma(16), dma(16), dma(2),
        ],
        compiler_params=pltpu.CompilerParams(
            collective_id=0, has_side_effects=True, vmem_limit_bytes=48 << 20
        ),
    )(hid, teacher_head, student_hidden, student_head, lab)
    z_hi = lax.axis_index("teacher") // 8
    ce = lax.dynamic_slice_in_dim(ce.reshape(16, 2, 16, 8), 8 * z_hi, 8, 2)
    agree = lax.dynamic_slice_in_dim(agree[0].reshape(2, 16, 8), 8 * z_hi, 8, 1)
    return (
        ce.transpose(2, 0, 1, 3).reshape(8, 16, 16),
        agree.transpose(1, 0, 2).reshape(8, 16),
        grad,
    )


def solution(mesh):
    return jax.shard_map(
        on_device,
        mesh=mesh,
        in_specs=(
            P("teacher", "vocab", None),
            P("teacher", "vocab"),
            P(None, "teacher"),
            P("teacher", "vocab"),
            P("teacher"),
        ),
        out_specs=(P("teacher", None, None), P("teacher", None), P("teacher", "vocab")),
        check_vma=False,
    )
```

```python
import jax
import jax.numpy as jnp
from jax import lax
from jax.experimental import pallas as pl
from jax.experimental.pallas import tpu as pltpu
from jax.sharding import PartitionSpec as P

HARD_SHARE = 0.3
MESH = pl.DeviceIdType.MESH
F32 = jnp.float32
BF16 = jnp.bfloat16
I32 = jnp.int32
PARTS = 2
ROWS = 128 // PARTS


def iota(shape, dim):
    return lax.broadcasted_iota(I32, shape, dim)


def row_token(r):
    return (r >> 3) & 15


def row_teacher(r):
    return (r >> 7) * 8 + (r & 7)


def fold_tokens(values):
    same = row_token(iota((256, 256), 0)) == row_token(iota((256, 256), 1))
    kept = jnp.where(same, values, 0.0).reshape(2, 16, 8, 256)
    return jnp.sum(kept, axis=1).reshape(16, 256)


def own_lane(values):
    same = iota((16, 256), 0) == row_teacher(iota((16, 256), 1))
    return jnp.sum(jnp.where(same, values, 0.0), axis=0, keepdims=True)


def kernel(
    hid_in, head, sh, shead_in, lab_in,
    grad_out, ce_out, agree_out,
    shead, W, hx, hid, L, Eb, Cb, mbuf, sbuf,
    S, Sc, A, Sx, T, Sz, SL, lab, yb, ys, xb, rb, gb, R,
    s_z, s_x, s_c, s_h1, s_h2, s_h3, s_st, s_y, s_ys, s_z1, s_z2, s_r,
    r_w, r_h1, r_h2, r_sc, r_sx, r_sz, r_lab, r_y, r_ys, r_z1, r_z2, r_r, l_w, l_in,
):
    t = lax.axis_index("teacher")
    v = lax.axis_index("vocab")
    zh, xc = t // 8, t % 8
    x, c = xc // 2, xc % 2
    zl, y = v // 4, v % 4
    z = zh * 8 + zl

    def dev(z_, xc_, y_):
        return {"teacher": (z_ // 8) * 8 + xc_, "vocab": (z_ % 8) * 4 + y_}

    def send(src, dst, ssem, rsem, to):
        pltpu.make_async_remote_copy(
            src_ref=src, dst_ref=dst, send_sem=ssem, recv_sem=rsem, device_id=to, device_id_type=MESH
        ).start()

    def done(ref, sem):
        pltpu.make_async_copy(ref, ref, sem).wait()

    def each(lo, hi, body):
        def step(i, carry):
            body(i)
            return carry
        lax.fori_loop(lo, hi, step, 0)

    z_to = lambda d: dev((z + d) % 16, xc, y)
    x_to = lambda d: dev(z, ((x + d) % 4) * 2 + c, y)
    y_to = lambda d: dev(z, xc, (y + d) % 4)
    xc_to = lambda d: dev(z, (xc + d) % 8, y)
    sibling = dev(z, x * 2 + 1 - c, y)
    partner = z_to(8)

    pltpu.make_async_copy(shead_in, shead, l_in.at[0]).start()
    barrier = pltpu.get_barrier_semaphore()
    each(1, 16, lambda d: pl.semaphore_signal(barrier, inc=1, device_id=z_to(d), device_id_type=MESH))
    each(1, 8, lambda d: pl.semaphore_signal(barrier, inc=1, device_id=xc_to(d), device_id_type=MESH))
    each(1, 4, lambda d: pl.semaphore_signal(barrier, inc=1, device_id=y_to(d), device_id_type=MESH))

    mine = pl.ds(pl.multiple_of(zh * 1024, 1024), 1024)
    other = pl.ds(pl.multiple_of((1 - zh) * 1024, 1024), 1024)
    piece = lambda zh_, x_, c_, part: ((zh_ * 8 + x_ * 2 + c_) * PARTS) + part
    w_at = lambda p: W.at[pl.ds(pl.multiple_of(p * ROWS, ROWS), ROWS), :]
    block = W.at[pl.ds(pl.multiple_of(t * 128, 128), 128), :]
    pltpu.make_async_copy(head.at[:, mine], block, l_w.at[0]).start()
    pltpu.make_async_copy(shead_in, shead, l_in.at[0]).wait()
    for k in range(4):
        cols = pl.ds(k * 512, 512)
        S[:, :, :, :, cols] = jnp.dot(sh[...], shead[:, cols], preferred_element_type=F32).reshape(2, 4, 2, 8, 512)
    lab[pl.ds(zh, 1)] = lab_in[...][None]
    pltpu.make_async_copy(head.at[:, mine], block, l_w.at[0]).wait()
    pl.semaphore_wait(barrier, 25)

    spread = (z % 4) * 2 + y // 2
    is_spread = xc == spread
    to_spread = dev(z, spread, y)

    @pl.when(is_spread)
    def _():
        pltpu.make_async_copy(hid_in, hx.at[xc], r_h1.at[xc]).start()

    @pl.when(jnp.logical_not(is_spread))
    def _():
        send(hid_in, hx.at[xc], s_h1.at[0], r_h1.at[xc], to_spread)

    carries = y // 2 == c

    def to_partner(part):
        p = piece(zh, x, c, part)
        send(head.at[pl.ds(pl.multiple_of(part * ROWS, ROWS), ROWS), other], w_at(p), s_z.at[part], r_w.at[p], partner)

    def along_x(zg, part):
        p = piece(zg, x, c, part)
        each(1, 4, lambda d: send(w_at(p), w_at(p), s_x.at[(zg * PARTS + part) * 3 + d - 1], r_w.at[p], x_to(d)))
        send(w_at(p), w_at(p), s_c.at[p], r_w.at[p], sibling)

    def from_x(zg):
        def go(i):
            p = piece(zg, (x + 1 + (i % 3) * 2 % 3) % 4, c, i // 3)
            done(w_at(p), r_w.at[p])
            send(w_at(p), w_at(p), s_c.at[p], r_w.at[p], sibling)
        each(0, 3 * PARTS, go)

    @pl.when(jnp.logical_not(carries))
    def _():
        each(0, PARTS, to_partner)
    each(0, PARTS, lambda part: along_x(zh, part))
    send(S.at[:, :, 1 - c], Sc, s_st.at[0], r_sc.at[0], sibling)

    k_spread = (z // 8) * 4 + ((z % 8) // 4) * 2 + y % 2

    def hid_at(k):
        return hid.at[pl.ds(pl.multiple_of(k * 32, 32), 32), :]

    @pl.when(is_spread)
    def _():
        each(0, 8, lambda i: done(hx.at[i], r_h1.at[i]))
        r, s = iota((128, 128), 0), iota((128, 128), 1)
        perm = ((s >> 4) == (r & 7)) & (((s >> 2) & 3) == (r >> 5)) & ((s & 3) == ((r >> 3) & 3))
        rows = jnp.dot(
            jnp.where(perm, 1.0, 0.0).astype(BF16), hx[...].reshape(128, 512), preferred_element_type=F32
        ).astype(BF16)
        for q in range(4):
            hid[pl.ds(pl.multiple_of(k_spread * 32, 32), 32), pl.ds(q * 512, 512)] = rows[q * 32:(q + 1) * 32]
        def go(i):
            d = (1 - i % 2) * (i // 2 + 1) + (i % 2) * (15 - i // 2)
            send(hid_at(k_spread), hid_at(k_spread), s_h2.at[i], r_h2.at[k_spread], z_to(d))
        each(0, 15, go)

    done(Sc, r_sc.at[0])
    for h in range(2):
        for x_ in range(4):
            A[x_, h] = S[h, x_, c] + Sc[h, x_]

    from_x(zh)
    each(1, 4, lambda d: send(A.at[(x + d) % 4], Sx.at[x], s_st.at[d], r_sx.at[x], x_to(d)))

    @pl.when(carries)
    def _():
        def go(k4):
            k = k4 * 2 + y % 2

            @pl.when(jnp.logical_not(jnp.logical_and(is_spread, k == k_spread)))
            def _():
                done(hid_at(k), r_h2.at[k])

            each(1, 4, lambda d: send(hid_at(k), hid_at(k), s_h3.at[k4 * 3 + d - 1], r_h2.at[k], y_to(d)))
        each(0, 4, go)
        each(0, PARTS, to_partner)

    each(1, 4, lambda d: done(Sx.at[(x + d) % 4], r_sx.at[(x + d) % 4]))
    total = A[x] + Sx[(x + 1) % 4] + Sx[(x + 2) % 4] + Sx[(x + 3) % 4]
    T[0] = total[:, :, :1024]
    T[1] = total[:, :, 1024:]

    def from_partner(part):
        p = piece(1 - zh, x, c, part)
        done(w_at(p), r_w.at[p])
        along_x(1 - zh, part)
    each(0, PARTS, from_partner)
    from_x(1 - zh)

    def last_hidden(k):
        @pl.when(jnp.logical_not(jnp.logical_and(y // 2 == c, y % 2 == k % 2)))
        def _():
            done(hid_at(k), r_h2.at[k])
    each(0, 8, last_hidden)

    def from_sibling(i):
        p = (i // PARTS) * (2 * PARTS) + (1 - c) * PARTS + i % PARTS
        done(w_at(p), r_w.at[p])
    each(0, 8 * PARTS, from_sibling)
    send(T.at[1 - zh], Sz, s_st.at[4], r_sz.at[0], partner)
    send(lab.at[zh], lab.at[zh], s_st.at[5], r_lab.at[0], partner)

    def scores(n):
        cols = pl.ds(pl.multiple_of(n * 256, 256), 256)
        L[:, cols] = jnp.dot(hid[...], W[:, cols], preferred_element_type=F32)
    each(0, 4, scores)

    def local_stats(n):
        rows = pl.ds(pl.multiple_of(n * 32, 32), 32)
        logits = L[rows, :]
        top = jnp.max(logits, axis=1, keepdims=True)
        low = logits - top
        e = jnp.exp(low)
        Eb[rows, :] = e.astype(BF16)
        Cb[rows, :] = low.astype(BF16)
        mbuf[rows, :] = jnp.broadcast_to(top, (32, 128))
        sbuf[rows, :] = jnp.broadcast_to(jnp.sum(e, axis=1, keepdims=True), (32, 128))
    each(0, 8, local_stats)

    cross = fold_tokens(lax.dot_general(
        Eb[...], Cb[...], (((1,), (1,)), ((), ())), preferred_element_type=F32))
    tops = mbuf[...]
    tops = fold_tokens(jnp.concatenate([tops, tops], axis=1))
    sums = sbuf[...]
    sums = fold_tokens(jnp.concatenate([sums, sums], axis=1))
    local_top = own_lane(tops)
    cross = cross + sums * local_top
    yb[y, 0:2] = cross.reshape(2, 8, 256)
    yb[y, 2:4] = jnp.concatenate([tops[:, :128], sums[:, 128:]], axis=1).reshape(2, 8, 256)
    each(1, 4, lambda d: send(yb.at[y], yb.at[y], s_y.at[d], r_y.at[y], y_to(d)))

    done(Sz, r_sz.at[0])
    student = (T[zh] + Sz[...]).reshape(16, 1024)
    SL[...] = student
    s_top = jnp.max(student, axis=1, keepdims=True)
    s_sum = jnp.sum(jnp.exp(student - s_top), axis=1, keepdims=True)
    mine_tok = row_token(iota((16, 128), 1)) == iota((16, 128), 0)
    s_top = jnp.sum(jnp.where(mine_tok, s_top, 0.0), axis=0, keepdims=True)
    s_sum = jnp.sum(jnp.where(mine_tok, s_sum, 0.0), axis=0, keepdims=True)
    ys[pl.ds(y, 1)] = jnp.concatenate([s_top, s_sum], axis=0)[None]
    each(1, 4, lambda d: send(ys.at[y], ys.at[y], s_ys.at[d], r_ys.at[y], y_to(d)))

    each(1, 4, lambda d: done(yb.at[(y + d) % 4], r_y.at[(y + d) % 4]))
    twice = lambda a: jnp.concatenate([a, a], axis=-1)
    got = yb[...]
    y_top = jnp.max(got[:, 2:4, :, :128], axis=0)
    y_scale = jnp.exp(got[:, 2:4, :, :128] - y_top[None])
    y_sum = jnp.sum(got[:, 2:4, :, 128:] * y_scale, axis=0)
    xb[:, 0, :] = jnp.sum(got[:, 0:2] * twice(y_scale), axis=0).reshape(16, 256)
    xb[:, 1, :] = jnp.concatenate([y_top, y_sum], axis=-1).reshape(16, 256)

    each(1, 16, lambda d: send(xb.at[(z + d) % 16], rb.at[z], s_z1.at[d], r_z1.at[z], z_to(d)))
    rb[pl.ds(z, 1)] = xb[pl.ds(z, 1)]
    each(1, 4, lambda d: done(ys.at[(y + d) % 4], r_ys.at[(y + d) % 4]))
    ytops, ysums = ys[:, 0, :], ys[:, 1, :]
    s_top = jnp.max(ytops, axis=0, keepdims=True)
    s_sum = jnp.sum(ysums * jnp.exp(ytops - s_top), axis=0, keepdims=True)
    each(1, 16, lambda d: done(rb.at[(z + d) % 16], r_z1.at[(z + d) % 16]))
    z_tops = rb[:, 1, :128]
    z_top = jnp.max(z_tops, axis=0, keepdims=True)
    z_scale = jnp.exp(z_tops - z_top)
    z_sum = jnp.sum(rb[:, 1, 128:] * z_scale, axis=0, keepdims=True)
    z_cross = jnp.sum(rb[:, 0, :] * twice(z_scale), axis=0, keepdims=True) / twice(z_sum)
    lane = iota((1, 256), 1)
    stud = jnp.where((lane & 1) == 0, twice(s_top), twice(s_sum))
    z_norm = jnp.where((lane >> 7) == z // 8, twice(z_top + jnp.log(z_sum)), stud)
    gb[pl.ds(z, 1)] = jnp.concatenate([z_cross, z_norm], axis=0)[None]
    each(1, 16, lambda d: send(gb.at[z], gb.at[z], s_z2.at[d], r_z2.at[z], z_to(d)))
    each(1, 16, lambda d: done(gb.at[(z + d) % 16], r_z2.at[(z + d) % 16]))
    norms = gb[:, 1, :]
    norm = own_lane(norms)
    ce = norm - gb[:, 0, :]
    ce_out[...] = ce
    inverse = 1.0 / (1.0 + jnp.sum(ce, axis=0, keepdims=True) / 16.0)
    r, l = iota((256, 256), 0), iota((256, 256), 1)
    by_row = jnp.sum(jnp.where(r == l, inverse, 0.0), axis=1, keepdims=True)
    share = jnp.sum(jnp.where(row_token(r) == row_token(l), by_row, 0.0), axis=0, keepdims=True)
    weights = inverse / share
    agree_out[...] = jnp.broadcast_to(weights * 16.0, (8, 256))
    scale = weights * jnp.exp(local_top - norm)
    spread_w = jnp.where(iota((16, 256), 0) == row_token(iota((16, 256), 1)), scale, 0.0)
    coarse = spread_w.astype(BF16)
    fine = (spread_w - coarse.astype(F32)).astype(BF16)
    soft = jnp.dot(coarse, Eb[...], preferred_element_type=F32) + jnp.dot(fine, Eb[...], preferred_element_type=F32)

    stud = jnp.concatenate([norms[:8, 128:], norms[8:, :128]], axis=0)
    stud_top = jnp.max(stud, axis=0, keepdims=True)
    stud_sums = pltpu.roll(stud, 127, 1)
    even = (iota((16, 128), 1) & 1) == 0
    stud_top = jnp.max(jnp.where(even, stud, -jnp.inf), axis=0, keepdims=True)
    stud_top = jnp.where(even[:1], stud_top, 0.0)
    stud_sum = jnp.sum(jnp.where(even, stud_sums * jnp.exp(jnp.where(even, stud - stud_top, 0.0)), 1.0), axis=0, keepdims=True)
    stud_norm = stud_top + jnp.log(stud_sum)

    done(lab.at[1 - zh], r_lab.at[0])
    lane = iota((16, 128), 1)
    first = (row_token(lane) == iota((16, 128), 0)) & ((lane & 7) == 0)
    s_norm = jnp.sum(jnp.where(first, stud_norm, 0.0), axis=1, keepdims=True)
    ids = lab[...].reshape(16, 128)
    ids = jnp.concatenate([ids] * 8, axis=1)
    onehot = jnp.where(iota((16, 1024), 1) + (v * 2048 + zh * 1024) == ids, HARD_SHARE, 0.0)
    residual = jnp.exp(SL[...] - s_norm) - ((1.0 - HARD_SHARE) * soft + onehot)
    R[zh, xc] = residual.astype(BF16)

    def pass_r(f, xc_, i, to):
        send(R.at[f, xc_], R.at[f, xc_], s_r.at[i], r_r.at[f * 8 + xc_], to)

    def await_r(f, xc_):
        done(R.at[f, xc_], r_r.at[f * 8 + xc_])

    pass_r(zh, xc, 0, partner)
    each(1, 4, lambda d: pass_r(zh, xc, d, x_to(d)))
    pass_r(zh, xc, 4, sibling)

    def relay_r(f, base):
        def go(d):
            xc_ = ((x + d) % 4) * 2 + c
            await_r(f, xc_)
            pass_r(f, xc_, base + d, sibling)
        each(1, 4, go)

    relay_r(zh, 4)
    tokens = sh[...].astype(F32).reshape(2, 8, 8, 128)
    tokens = jnp.swapaxes(tokens, 0, 1).reshape(128, 128).astype(BF16)
    await_r(1 - zh, xc)
    each(1, 4, lambda d: pass_r(1 - zh, xc, 7 + d, x_to(d)))
    pass_r(1 - zh, xc, 11, sibling)
    relay_r(1 - zh, 11)
    for f in range(2):
        each(0, 4, lambda i: await_r(f, i * 2 + 1 - c))
    for f in range(2):
        for k in range(2):
            grad_out[:, pl.ds(f * 1024 + k * 512, 512)] = lax.dot_general(
                tokens, R[f, :, :, pl.ds(k * 512, 512)].reshape(128, 512),
                (((0,), (0,)), ((), ())), preferred_element_type=F32)

    each(0, PARTS, lambda i: done(w_at(0), s_z.at[i]))
    each(0, 6 * PARTS, lambda i: done(w_at(0), s_x.at[i]))

    def own_core(i):
        p = (i // PARTS) * (2 * PARTS) + c * PARTS + i % PARTS
        done(w_at(p), s_c.at[p])
    each(0, 8 * PARTS, own_core)

    @pl.when(jnp.logical_not(is_spread))
    def _():
        done(hx.at[0], s_h1.at[0])

    @pl.when(is_spread)
    def _():
        each(0, 15, lambda d: done(hid_at(0), s_h2.at[d]))

    @pl.when(y // 2 == c)
    def _():
        each(0, 12, lambda i: done(hid_at(0), s_h3.at[i]))
    done(Sc, s_st.at[0])
    each(1, 4, lambda d: done(A.at[0], s_st.at[d]))
    done(Sz, s_st.at[4])
    done(lab.at[0], s_st.at[5])
    each(1, 4, lambda d: done(yb.at[0], s_y.at[d]))
    each(1, 4, lambda d: done(ys.at[0], s_ys.at[d]))
    each(1, 16, lambda d: done(rb.at[0], s_z1.at[d]))
    each(1, 16, lambda d: done(gb.at[0], s_z2.at[d]))
    each(0, 15, lambda i: done(R.at[0, 0], s_r.at[i]))


def on_device(teacher_hidden, teacher_head, student_hidden, student_head, labels):
    hid = teacher_hidden[0].reshape(4, 4, 512).transpose(1, 0, 2).reshape(16, 512)
    lab = jnp.broadcast_to(labels[:, None], (8, 128))
    vmem = lambda shape, dtype=F32: pltpu.VMEM(shape, dtype)
    dma = lambda n: pltpu.SemaphoreType.DMA((n,))
    space = pl.BlockSpec(memory_space=pltpu.VMEM)
    hbm = pl.BlockSpec(memory_space=pl.ANY)
    grad, ce, agree = pl.pallas_call(
        kernel,
        out_shape=(
            jax.ShapeDtypeStruct((128, 2048), F32),
            jax.ShapeDtypeStruct((16, 256), F32),
            jax.ShapeDtypeStruct((8, 256), F32),
        ),
        in_specs=[space, hbm, space, hbm, space],
        out_specs=(space,) * 3,
        scratch_shapes=[
            vmem((128, 2048), BF16), vmem((2048, 1024), BF16), vmem((8, 16, 512), BF16), vmem((256, 2048), BF16),
            vmem((256, 1024)), vmem((256, 1024), BF16), vmem((256, 1024), BF16), vmem((256, 128)), vmem((256, 128)),
            vmem((2, 4, 2, 8, 2048)), vmem((2, 4, 8, 2048)), vmem((4, 2, 8, 2048)), vmem((4, 2, 8, 2048)),
            vmem((2, 2, 8, 1024)), vmem((2, 8, 1024)), vmem((16, 1024)), vmem((2, 8, 128), I32),
            vmem((4, 4, 8, 256)), vmem((4, 2, 128)), vmem((16, 2, 256)), vmem((16, 2, 256)), vmem((16, 2, 256)),
            vmem((2, 8, 16, 1024), BF16),
            dma(PARTS), dma(6 * PARTS), dma(16 * PARTS), dma(1), dma(16), dma(12), dma(6), dma(4), dma(4), dma(16), dma(16), dma(15),
            dma(16 * PARTS), dma(8), dma(8), dma(1), dma(4), dma(1), dma(1), dma(4), dma(4), dma(16), dma(16), dma(16), dma(1), dma(1),
        ],
        compiler_params=pltpu.CompilerParams(
            collective_id=0, has_side_effects=True, vmem_limit_bytes=48 << 20
        ),
    )(hid, teacher_head, student_hidden, student_head, lab)
    z_hi = lax.axis_index("teacher") // 8
    ce = lax.dynamic_slice_in_dim(ce.reshape(16, 2, 16, 8), 8 * z_hi, 8, 2)
    agree = lax.dynamic_slice_in_dim(agree[0].reshape(2, 16, 8), 8 * z_hi, 8, 1)
    return (
        ce.transpose(2, 0, 1, 3).reshape(8, 16, 16),
        agree.transpose(1, 0, 2).reshape(8, 16),
        grad,
    )


def solution(mesh):
    return jax.shard_map(
        on_device,
        mesh=mesh,
        in_specs=(
            P("teacher", "vocab", None),
            P("teacher", "vocab"),
            P(None, "teacher"),
            P("teacher", "vocab"),
            P("teacher"),
        ),
        out_specs=(P("teacher", None, None), P("teacher", None), P("teacher", "vocab")),
        check_vma=False,
    )
```

```python
import jax
import jax.numpy as jnp
from jax import lax
from jax.experimental import pallas as pl
from jax.experimental.pallas import tpu as pltpu
from jax.sharding import PartitionSpec as P

HARD_SHARE = 0.3
MESH = pl.DeviceIdType.MESH
F32 = jnp.float32
BF16 = jnp.bfloat16
I32 = jnp.int32
PARTS = 2
ROWS = 128 // PARTS
WINDOW = 2


def iota(shape, dim):
    return lax.broadcasted_iota(I32, shape, dim)


def row_token(r):
    return (r >> 3) & 15


def row_teacher(r):
    return (r >> 7) * 8 + (r & 7)


def fold_tokens(values):
    same = row_token(iota((256, 256), 0)) == row_token(iota((256, 256), 1))
    kept = jnp.where(same, values, 0.0).reshape(2, 16, 8, 256)
    return jnp.sum(kept, axis=1).reshape(16, 256)


def own_lane(values):
    same = iota((16, 256), 0) == row_teacher(iota((16, 256), 1))
    return jnp.sum(jnp.where(same, values, 0.0), axis=0, keepdims=True)


div, rem = lax.div, lax.rem


def kernel(
    hid_in, head, sh, shead_in, lab_in,
    grad_out, ce_out, agree_out,
    shead, W, hx, hid, L, Eb, Cb, mbuf, sbuf,
    S, Sc, A, Sx, T, Sz, SL, lab, yb, ys, xb, rb, gb, R,
    s_z, s_x, s_c, s_h1, s_h2, s_h3, s_st, s_y, s_ys, s_z1, s_z2, s_r,
    r_w, r_h1, r_h2, r_sc, r_sx, r_sz, r_lab, r_y, r_ys, r_z1, r_z2, r_r, l_w, l_in,
):
    t = lax.axis_index("teacher")
    v = lax.axis_index("vocab")
    zh, xc = div(t, 8), rem(t, 8)
    x, c = div(xc, 2), rem(xc, 2)
    zl, y = div(v, 4), rem(v, 4)
    z = zh * 8 + zl

    def dev(z_, xc_, y_):
        return {"teacher": div(z_, 8) * 8 + xc_, "vocab": rem(z_, 8) * 4 + y_}

    def send(src, dst, ssem, rsem, to):
        pltpu.make_async_remote_copy(
            src_ref=src, dst_ref=dst, send_sem=ssem, recv_sem=rsem, device_id=to, device_id_type=MESH
        ).start()

    def done(ref, sem):
        pltpu.make_async_copy(ref, ref, sem).wait()

    def each(lo, hi, body):
        def step(i, carry):
            body(i)
            return carry
        lax.fori_loop(lo, hi, step, 0)

    z_to = lambda d: dev(rem(z + d, 16), xc, y)
    x_to = lambda d: dev(z, rem(x + d, 4) * 2 + c, y)
    y_to = lambda d: dev(z, xc, rem(y + d, 4))
    xc_to = lambda d: dev(z, rem(xc + d, 8), y)
    sibling = dev(z, x * 2 + 1 - c, y)
    partner = z_to(8)

    pltpu.make_async_copy(shead_in, shead, l_in.at[0]).start()
    barrier = pltpu.get_barrier_semaphore()
    each(1, 16, lambda d: pl.semaphore_signal(barrier, inc=1, device_id=z_to(d), device_id_type=MESH))
    each(1, 8, lambda d: pl.semaphore_signal(barrier, inc=1, device_id=xc_to(d), device_id_type=MESH))
    each(1, 4, lambda d: pl.semaphore_signal(barrier, inc=1, device_id=y_to(d), device_id_type=MESH))

    mine = pl.ds(pl.multiple_of(zh * 1024, 1024), 1024)
    other = pl.ds(pl.multiple_of((1 - zh) * 1024, 1024), 1024)
    piece = lambda zh_, x_, c_, part: ((zh_ * 8 + x_ * 2 + c_) * PARTS) + part
    w_at = lambda p: W.at[pl.ds(pl.multiple_of(p * ROWS, ROWS), ROWS), :]
    block = W.at[pl.ds(pl.multiple_of(t * 128, 128), 128), :]
    pltpu.make_async_copy(head.at[:, mine], block, l_w.at[0]).start()
    pltpu.make_async_copy(shead_in, shead, l_in.at[0]).wait()
    for k in range(4):
        cols = pl.ds(k * 512, 512)
        S[:, :, :, :, cols] = jnp.dot(sh[...], shead[:, cols], preferred_element_type=F32).reshape(2, 4, 2, 8, 512)
    lab[pl.ds(zh, 1)] = lab_in[...][None]
    pltpu.make_async_copy(head.at[:, mine], block, l_w.at[0]).wait()
    pl.semaphore_wait(barrier, 25)

    spread = rem(z, 4) * 2 + div(y, 2)
    is_spread = xc == spread
    to_spread = dev(z, spread, y)

    @pl.when(is_spread)
    def _():
        pltpu.make_async_copy(hid_in, hx.at[xc], r_h1.at[xc]).start()

    @pl.when(jnp.logical_not(is_spread))
    def _():
        send(hid_in, hx.at[xc], s_h1.at[0], r_h1.at[xc], to_spread)

    carries = div(y, 2) == c

    def to_partner(part):
        p = piece(zh, x, c, part)
        send(head.at[pl.ds(pl.multiple_of(part * ROWS, ROWS), ROWS), other], w_at(p), s_z.at[0], r_w.at[p], partner)

    def along_x(zg, part):
        p = piece(zg, x, c, part)
        each(1, 4, lambda d: send(w_at(p), w_at(p), s_x.at[0], r_w.at[p], x_to(d)))
        send(w_at(p), w_at(p), s_c.at[0], r_w.at[p], sibling)

    def from_x(zg, part):
        def go(i):
            p = piece(zg, rem(x + 1 + rem(i * 2, 3), 4), c, part)
            done(w_at(p), r_w.at[p])
            send(w_at(p), w_at(p), s_c.at[0], r_w.at[p], sibling)
        each(0, 3, go)

    @pl.when(jnp.logical_not(carries))
    def _():
        each(0, WINDOW, to_partner)

    @pl.when(carries)
    def _():
        to_partner(0)
    each(0, PARTS, lambda part: along_x(zh, part))
    send(S.at[:, :, 1 - c], Sc, s_st.at[0], r_sc.at[0], sibling)

    k_spread = div(z, 4) * 2 + rem(y, 2)

    def hid_at(k):
        return hid.at[pl.ds(pl.multiple_of(k * 32, 32), 32), :]

    def beside(k4, k):
        send(hid_at(k), hid_at(k), s_h2.at[0], r_h2.at[k], z_to(1))
        send(hid_at(k), hid_at(k), s_h2.at[0], r_h2.at[k], z_to(15))

    @pl.when(is_spread)
    def _():
        each(0, 8, lambda i: done(hx.at[i], r_h1.at[i]))
        r, s = iota((128, 128), 0), iota((128, 128), 1)
        perm = ((s >> 4) == (r & 7)) & (((s >> 2) & 3) == (r >> 5)) & ((s & 3) == ((r >> 3) & 3))
        rows = jnp.dot(
            jnp.where(perm, 1.0, 0.0).astype(BF16), hx[...].reshape(128, 512), preferred_element_type=F32
        ).astype(BF16)
        for q in range(4):
            hid[pl.ds(pl.multiple_of(k_spread * 32, 32), 32), pl.ds(q * 512, 512)] = rows[q * 32:(q + 1) * 32]
        for i, d in enumerate((4, 12, 8)):
            send(hid_at(k_spread), hid_at(k_spread), s_h2.at[0], r_h2.at[k_spread], z_to(d))
        beside(div(z, 4), k_spread)

    done(Sc, r_sc.at[0])
    for h in range(2):
        for x_ in range(4):
            A[x_, h] = S[h, x_, c] + Sc[h, x_]

    each(0, PARTS, lambda part: from_x(zh, part))
    each(1, 4, lambda d: send(A.at[rem(x + d, 4)], Sx.at[x], s_st.at[1], r_sx.at[x], x_to(d)))

    place = rem(z + 16 - x, 4)

    @pl.when(carries)
    def _():
        def go(i):
            k4 = rem(div(z + 17 - x, 4) + i + div(i, 2) * (1 - 2 * rem(i, 2)), 4)
            k = k4 * 2 + rem(y, 2)
            own = jnp.logical_and(is_spread, k == k_spread)

            @pl.when(jnp.logical_not(own))
            def _():
                done(hid_at(k), r_h2.at[k])

            @pl.when(jnp.logical_and(is_spread, k != k_spread))
            def _():
                beside(k4, k)

            @pl.when(jnp.logical_and(place == 1, rem(k4, 2) == 0))
            def _():
                send(hid_at(k), hid_at(k), s_h2.at[0], r_h2.at[k], z_to(1))

            @pl.when(jnp.logical_and(place == 3, rem(k4, 2) == 1))
            def _():
                send(hid_at(k), hid_at(k), s_h2.at[0], r_h2.at[k], z_to(15))

            each(1, 4, lambda d: send(hid_at(k), hid_at(k), s_h3.at[0], r_h2.at[k], y_to(d)))
        each(0, 4, go)
        to_partner(1)

    each(1, 4, lambda d: done(Sx.at[rem(x + d, 4)], r_sx.at[rem(x + d, 4)]))
    total = A[x] + Sx[rem(x + 1, 4)] + Sx[rem(x + 2, 4)] + Sx[rem(x + 3, 4)]
    T[0] = total[:, :, :1024]
    T[1] = total[:, :, 1024:]

    for part in range(PARTS):
        p = piece(1 - zh, x, c, part)
        done(w_at(p), r_w.at[p])
        if part + WINDOW < PARTS:
            to_partner(part + WINDOW)
        along_x(1 - zh, part)
        if part > 0:
            from_x(1 - zh, part - 1)
    send(T.at[1 - zh], Sz, s_st.at[4], r_sz.at[0], partner)
    send(lab.at[zh], lab.at[zh], s_st.at[5], r_lab.at[0], partner)
    from_x(1 - zh, PARTS - 1)

    def last_hidden(k):
        @pl.when(jnp.logical_not(jnp.logical_and(carries, rem(y, 2) == rem(k, 2))))
        def _():
            done(hid_at(k), r_h2.at[k])
    each(0, 8, last_hidden)

    def from_sibling(i):
        p = div(i, PARTS) * (2 * PARTS) + (1 - c) * PARTS + rem(i, PARTS)
        done(w_at(p), r_w.at[p])
    each(0, 8 * PARTS, from_sibling)

    def scores(n):
        cols = pl.ds(pl.multiple_of(n * 256, 256), 256)
        L[:, cols] = jnp.dot(hid[...], W[:, cols], preferred_element_type=F32)
    each(0, 4, scores)

    def local_stats(n):
        rows = pl.ds(pl.multiple_of(n * 32, 32), 32)
        logits = L[rows, :]
        top = jnp.max(logits, axis=1, keepdims=True)
        low = logits - top
        e = jnp.exp(low)
        Eb[rows, :] = e.astype(BF16)
        Cb[rows, :] = low.astype(BF16)
        mbuf[rows, :] = jnp.broadcast_to(top, (32, 128))
        sbuf[rows, :] = jnp.broadcast_to(jnp.sum(e, axis=1, keepdims=True), (32, 128))
    each(0, 8, local_stats)

    cross = fold_tokens(lax.dot_general(
        Eb[...], Cb[...], (((1,), (1,)), ((), ())), preferred_element_type=F32))
    tops = mbuf[...]
    tops = fold_tokens(jnp.concatenate([tops, tops], axis=1))
    sums = sbuf[...]
    sums = fold_tokens(jnp.concatenate([sums, sums], axis=1))
    local_top = own_lane(tops)
    cross = cross + sums * local_top
    yb[y, 0:2] = cross.reshape(2, 8, 256)
    yb[y, 2:4] = jnp.concatenate([tops[:, :128], sums[:, 128:]], axis=1).reshape(2, 8, 256)
    each(1, 4, lambda d: send(yb.at[y], yb.at[y], s_y.at[0], r_y.at[y], y_to(d)))

    done(Sz, r_sz.at[0])
    student = (T[zh] + Sz[...]).reshape(16, 1024)
    SL[...] = student
    s_top = jnp.max(student, axis=1, keepdims=True)
    s_sum = jnp.sum(jnp.exp(student - s_top), axis=1, keepdims=True)
    mine_tok = row_token(iota((16, 128), 1)) == iota((16, 128), 0)
    s_top = jnp.sum(jnp.where(mine_tok, s_top, 0.0), axis=0, keepdims=True)
    s_sum = jnp.sum(jnp.where(mine_tok, s_sum, 0.0), axis=0, keepdims=True)
    ys[pl.ds(y, 1)] = jnp.concatenate([s_top, s_sum], axis=0)[None]
    each(1, 4, lambda d: send(ys.at[y], ys.at[y], s_ys.at[0], r_ys.at[y], y_to(d)))

    each(1, 4, lambda d: done(yb.at[rem(y + d, 4)], r_y.at[rem(y + d, 4)]))
    twice = lambda a: jnp.concatenate([a, a], axis=-1)
    got = yb[...]
    y_top = jnp.max(got[:, 2:4, :, :128], axis=0)
    y_scale = jnp.exp(got[:, 2:4, :, :128] - y_top[None])
    y_sum = jnp.sum(got[:, 2:4, :, 128:] * y_scale, axis=0)
    xb[:, 0, :] = jnp.sum(got[:, 0:2] * twice(y_scale), axis=0).reshape(16, 256)
    xb[:, 1, :] = jnp.concatenate([y_top, y_sum], axis=-1).reshape(16, 256)

    def first_sends_left():
        done(W.at[pl.ds(0, 128), :], s_z.at[0])
        done(W.at[pl.ds(0, 768), :], s_x.at[0])
        done(W.at[pl.ds(0, 1024), :], s_c.at[0])

        @pl.when(jnp.logical_not(is_spread))
        def _():
            done(hx.at[0], s_h1.at[0])

        @pl.when(is_spread)
        def _():
            done(W.at[pl.ds(0, 11 * 64), :], s_h2.at[0])

        @pl.when(jnp.logical_and(carries, rem(place, 2) == 1))
        def _():
            done(W.at[pl.ds(0, 2 * 64), :], s_h2.at[0])

        @pl.when(carries)
        def _():
            done(W.at[pl.ds(0, 12 * 64), :], s_h3.at[0])
        done(Sc, s_st.at[0])
        done(A.at[pl.ds(0, 3)], s_st.at[1])
        done(Sz, s_st.at[4])
        done(lab.at[0], s_st.at[5])
        done(yb.at[pl.ds(0, 3)], s_y.at[0])
        done(ys.at[pl.ds(0, 3)], s_ys.at[0])

    each(1, 16, lambda d: send(xb.at[rem(z + d, 16)], rb.at[z], s_z1.at[0], r_z1.at[0], z_to(d)))
    first_sends_left()
    rb[pl.ds(z, 1)] = xb[pl.ds(z, 1)]
    each(1, 4, lambda d: done(ys.at[rem(y + d, 4)], r_ys.at[rem(y + d, 4)]))
    ytops, ysums = ys[:, 0, :], ys[:, 1, :]
    s_top = jnp.max(ytops, axis=0, keepdims=True)
    s_sum = jnp.sum(ysums * jnp.exp(ytops - s_top), axis=0, keepdims=True)
    done(rb.at[pl.ds(0, 15)], r_z1.at[0])
    z_tops = rb[:, 1, :128]
    z_top = jnp.max(z_tops, axis=0, keepdims=True)
    z_scale = jnp.exp(z_tops - z_top)
    z_sum = jnp.sum(rb[:, 1, 128:] * z_scale, axis=0, keepdims=True)
    z_cross = jnp.sum(rb[:, 0, :] * twice(z_scale), axis=0, keepdims=True) / twice(z_sum)
    lane = iota((1, 256), 1)
    stud = jnp.where((lane & 1) == 0, twice(s_top), twice(s_sum))
    z_norm = jnp.where((lane >> 7) == zh, twice(z_top + jnp.log(z_sum)), stud)
    gb[pl.ds(z, 1)] = jnp.concatenate([z_cross, z_norm], axis=0)[None]
    each(1, 16, lambda d: send(gb.at[z], gb.at[z], s_z2.at[0], r_z2.at[0], z_to(d)))
    done(gb.at[pl.ds(0, 15)], r_z2.at[0])
    norms = gb[:, 1, :]
    norm = own_lane(norms)
    ce = norm - gb[:, 0, :]
    ce_out[...] = ce
    inverse = 1.0 / (1.0 + jnp.sum(ce, axis=0, keepdims=True) / 16.0)
    r, l = iota((256, 256), 0), iota((256, 256), 1)
    by_row = jnp.sum(jnp.where(r == l, inverse, 0.0), axis=1, keepdims=True)
    share = jnp.sum(jnp.where(row_token(r) == row_token(l), by_row, 0.0), axis=0, keepdims=True)
    weights = inverse / share
    agree_out[...] = jnp.broadcast_to(weights * 16.0, (8, 256))
    scale = weights * jnp.exp(local_top - norm)
    spread_w = jnp.where(iota((16, 256), 0) == row_token(iota((16, 256), 1)), scale, 0.0)
    coarse = spread_w.astype(BF16)
    fine = (spread_w - coarse.astype(F32)).astype(BF16)
    soft = jnp.dot(coarse, Eb[...], preferred_element_type=F32) + jnp.dot(fine, Eb[...], preferred_element_type=F32)

    stud = jnp.concatenate([norms[:8, 128:], norms[8:, :128]], axis=0)
    stud_top = jnp.max(stud, axis=0, keepdims=True)
    stud_sums = pltpu.roll(stud, 127, 1)
    even = (iota((16, 128), 1) & 1) == 0
    stud_top = jnp.max(jnp.where(even, stud, -jnp.inf), axis=0, keepdims=True)
    stud_top = jnp.where(even[:1], stud_top, 0.0)
    stud_sum = jnp.sum(jnp.where(even, stud_sums * jnp.exp(jnp.where(even, stud - stud_top, 0.0)), 1.0), axis=0, keepdims=True)
    stud_norm = stud_top + jnp.log(stud_sum)

    done(lab.at[1 - zh], r_lab.at[0])
    lane = iota((16, 128), 1)
    first = (row_token(lane) == iota((16, 128), 0)) & ((lane & 7) == 0)
    s_norm = jnp.sum(jnp.where(first, stud_norm, 0.0), axis=1, keepdims=True)
    ids = lab[...].reshape(16, 128)
    ids = jnp.concatenate([ids] * 8, axis=1)
    onehot = jnp.where(iota((16, 1024), 1) + (v * 2048 + zh * 1024) == ids, HARD_SHARE, 0.0)
    residual = jnp.exp(SL[...] - s_norm) - ((1.0 - HARD_SHARE) * soft + onehot)
    R[zh, xc] = residual.astype(BF16)

    def pass_r(f, xc_, i, to):
        send(R.at[f, xc_], R.at[f, xc_], s_r.at[0], r_r.at[f * 8 + xc_], to)

    def await_r(f, xc_):
        done(R.at[f, xc_], r_r.at[f * 8 + xc_])

    pass_r(zh, xc, 0, partner)
    each(1, 4, lambda d: pass_r(zh, xc, d, x_to(d)))
    pass_r(zh, xc, 4, sibling)

    def relay_r(f, base):
        def go(d):
            xc_ = (rem(x + d, 4)) * 2 + c
            await_r(f, xc_)
            pass_r(f, xc_, base + d, sibling)
        each(1, 4, go)

    relay_r(zh, 4)
    tokens = sh[...].astype(F32).reshape(2, 8, 8, 128)
    tokens = jnp.swapaxes(tokens, 0, 1).reshape(128, 128).astype(BF16)
    await_r(1 - zh, xc)
    each(1, 4, lambda d: pass_r(1 - zh, xc, 7 + d, x_to(d)))
    pass_r(1 - zh, xc, 11, sibling)
    relay_r(1 - zh, 11)
    for f in range(2):
        each(0, 4, lambda i: await_r(f, i * 2 + 1 - c))
    for f in range(2):
        for k in range(2):
            grad_out[:, pl.ds(f * 1024 + k * 512, 512)] = lax.dot_general(
                tokens, R[f, :, :, pl.ds(k * 512, 512)].reshape(128, 512),
                (((0,), (0,)), ((), ())), preferred_element_type=F32)

    done(xb.at[pl.ds(0, 15)], s_z1.at[0])
    done(gb.at[pl.ds(0, 15)], s_z2.at[0])
    done(W.at[pl.ds(0, 240), :], s_r.at[0])


def on_device(teacher_hidden, teacher_head, student_hidden, student_head, labels):
    hid = teacher_hidden[0].reshape(4, 4, 512).transpose(1, 0, 2).reshape(16, 512)
    lab = jnp.broadcast_to(labels[:, None], (8, 128))
    vmem = lambda shape, dtype=F32: pltpu.VMEM(shape, dtype)
    dma = lambda n: pltpu.SemaphoreType.DMA((n,))
    space = pl.BlockSpec(memory_space=pltpu.VMEM)
    hbm = pl.BlockSpec(memory_space=pl.ANY)
    grad, ce, agree = pl.pallas_call(
        kernel,
        out_shape=(
            jax.ShapeDtypeStruct((128, 2048), F32),
            jax.ShapeDtypeStruct((16, 256), F32),
            jax.ShapeDtypeStruct((8, 256), F32),
        ),
        in_specs=[space, hbm, space, hbm, space],
        out_specs=(space,) * 3,
        scratch_shapes=[
            vmem((128, 2048), BF16), vmem((2048, 1024), BF16), vmem((8, 16, 512), BF16), vmem((256, 2048), BF16),
            vmem((256, 1024)), vmem((256, 1024), BF16), vmem((256, 1024), BF16), vmem((256, 128)), vmem((256, 128)),
            vmem((2, 4, 2, 8, 2048)), vmem((2, 4, 8, 2048)), vmem((4, 2, 8, 2048)), vmem((4, 2, 8, 2048)),
            vmem((2, 2, 8, 1024)), vmem((2, 8, 1024)), vmem((16, 1024)), vmem((2, 8, 128), I32),
            vmem((4, 4, 8, 256)), vmem((4, 2, 128)), vmem((16, 2, 256)), vmem((16, 2, 256)), vmem((16, 2, 256)),
            vmem((2, 8, 16, 1024), BF16),
            dma(1), dma(1), dma(1), dma(1), dma(1), dma(1), dma(6), dma(1), dma(1), dma(1), dma(1), dma(1),
            dma(16 * PARTS), dma(8), dma(8), dma(1), dma(4), dma(1), dma(1), dma(4), dma(4), dma(1), dma(1), dma(16),
            dma(1), dma(1),
        ],
        compiler_params=pltpu.CompilerParams(
            collective_id=0, has_side_effects=True, vmem_limit_bytes=48 << 20
        ),
    )(hid, teacher_head, student_hidden, student_head, lab)
    z_hi = lax.axis_index("teacher") // 8
    ce = lax.dynamic_slice_in_dim(ce.reshape(16, 2, 16, 8), 8 * z_hi, 8, 2)
    agree = lax.dynamic_slice_in_dim(agree[0].reshape(2, 16, 8), 8 * z_hi, 8, 1)
    return (
        ce.transpose(2, 0, 1, 3).reshape(8, 16, 16),
        agree.transpose(1, 0, 2).reshape(8, 16),
        grad,
    )


def solution(mesh):
    return jax.shard_map(
        on_device,
        mesh=mesh,
        in_specs=(
            P("teacher", "vocab", None),
            P("teacher", "vocab"),
            P(None, "teacher"),
            P("teacher", "vocab"),
            P("teacher"),
        ),
        out_specs=(P("teacher", None, None), P("teacher", None), P("teacher", "vocab")),
        check_vma=False,
    )
```

```python
import jax
import jax.numpy as jnp
from jax import lax
from jax.experimental import pallas as pl
from jax.experimental.pallas import tpu as pltpu
from jax.sharding import PartitionSpec as P

HARD_SHARE = 0.3
MESH = pl.DeviceIdType.MESH
F32 = jnp.float32
BF16 = jnp.bfloat16
I32 = jnp.int32
PARTS = 2
ROWS = 128 // PARTS
WINDOW = 2


def iota(shape, dim):
    return lax.broadcasted_iota(I32, shape, dim)


def row_token(r):
    return (r >> 3) & 15


def row_teacher(r):
    return (r >> 7) * 8 + (r & 7)


def fold_tokens(values):
    same = row_token(iota((256, 256), 0)) == row_token(iota((256, 256), 1))
    kept = jnp.where(same, values, 0.0).reshape(2, 16, 8, 256)
    return jnp.sum(kept, axis=1).reshape(16, 256)


def own_lane(values):
    same = iota((16, 256), 0) == row_teacher(iota((16, 256), 1))
    return jnp.sum(jnp.where(same, values, 0.0), axis=0, keepdims=True)


div, rem = lax.div, lax.rem


def kernel(
    hid_in, head, sh, shead_in, lab_in,
    grad_out, ce_out, agree_out,
    shead, W, hx, hid, L, Eb, Cb, mbuf, sbuf,
    S, Sc, A, Sx, T, Sz, SL, lab, yb, ys, xb, rb, gb, R,
    s_z, s_x, s_c, s_h1, s_h2, s_h3, s_st, s_y, s_ys, s_z1, s_z2, s_r,
    r_w, r_h1, r_h2, r_sc, r_sx, r_sz, r_lab, r_y, r_ys, r_z1, r_z2, r_r, l_w, l_in,
):
    t = lax.axis_index("teacher")
    v = lax.axis_index("vocab")
    zh, xc = div(t, 8), rem(t, 8)
    x, c = div(xc, 2), rem(xc, 2)
    zl, y = div(v, 4), rem(v, 4)
    z = zh * 8 + zl

    def dev(z_, xc_, y_):
        return {"teacher": div(z_, 8) * 8 + xc_, "vocab": rem(z_, 8) * 4 + y_}

    def send(src, dst, ssem, rsem, to):
        pltpu.make_async_remote_copy(
            src_ref=src, dst_ref=dst, send_sem=ssem, recv_sem=rsem, device_id=to, device_id_type=MESH
        ).start()

    def done(ref, sem):
        pltpu.make_async_copy(ref, ref, sem).wait()

    def each(lo, hi, body):
        def step(i, carry):
            body(i)
            return carry
        lax.fori_loop(lo, hi, step, 0)

    def far_first(body):
        each(0, 15, lambda i: body(8 + div(i, 2) * (1 - 2 * rem(i, 2)) - rem(i, 2)))

    z_to = lambda d: dev(rem(z + d, 16), xc, y)
    x_to = lambda d: dev(z, rem(x + d, 4) * 2 + c, y)
    y_to = lambda d: dev(z, xc, rem(y + d, 4))
    xc_to = lambda d: dev(z, rem(xc + d, 8), y)
    sibling = dev(z, x * 2 + 1 - c, y)
    partner = z_to(8)

    pltpu.make_async_copy(shead_in, shead, l_in.at[0]).start()
    barrier = pltpu.get_barrier_semaphore()
    each(1, 16, lambda d: pl.semaphore_signal(barrier, inc=1, device_id=z_to(d), device_id_type=MESH))
    each(1, 8, lambda d: pl.semaphore_signal(barrier, inc=1, device_id=xc_to(d), device_id_type=MESH))
    each(1, 4, lambda d: pl.semaphore_signal(barrier, inc=1, device_id=y_to(d), device_id_type=MESH))

    mine = pl.ds(pl.multiple_of(zh * 1024, 1024), 1024)
    other = pl.ds(pl.multiple_of((1 - zh) * 1024, 1024), 1024)
    piece = lambda zh_, x_, c_, part: ((zh_ * 8 + x_ * 2 + c_) * PARTS) + part
    w_at = lambda p: W.at[pl.ds(pl.multiple_of(p * ROWS, ROWS), ROWS), :]
    block = W.at[pl.ds(pl.multiple_of(t * 128, 128), 128), :]
    pltpu.make_async_copy(head.at[:, mine], block, l_w.at[0]).start()
    pltpu.make_async_copy(shead_in, shead, l_in.at[0]).wait()
    for k in range(4):
        cols = pl.ds(k * 512, 512)
        S[:, :, :, :, cols] = jnp.dot(sh[...], shead[:, cols], preferred_element_type=F32).reshape(2, 4, 2, 8, 512)
    lab[pl.ds(zh, 1)] = lab_in[...][None]
    pltpu.make_async_copy(head.at[:, mine], block, l_w.at[0]).wait()
    pl.semaphore_wait(barrier, 25)

    spread = rem(z, 4) * 2 + div(y, 2)
    is_spread = xc == spread
    to_spread = dev(z, spread, y)

    @pl.when(is_spread)
    def _():
        pltpu.make_async_copy(hid_in, hx.at[xc], r_h1.at[xc]).start()

    @pl.when(jnp.logical_not(is_spread))
    def _():
        send(hid_in, hx.at[xc], s_h1.at[0], r_h1.at[xc], to_spread)

    carries = div(y, 2) == c

    def to_partner(part):
        p = piece(zh, x, c, part)
        send(head.at[pl.ds(pl.multiple_of(part * ROWS, ROWS), ROWS), other], w_at(p), s_z.at[0], r_w.at[p], partner)

    def along_x(zg, part):
        p = piece(zg, x, c, part)
        each(1, 4, lambda d: send(w_at(p), w_at(p), s_x.at[0], r_w.at[p], x_to(d)))
        send(w_at(p), w_at(p), s_c.at[0], r_w.at[p], sibling)

    def from_x(zg, part):
        def go(i):
            p = piece(zg, rem(x + 1 + rem(i * 2, 3), 4), c, part)
            done(w_at(p), r_w.at[p])
            send(w_at(p), w_at(p), s_c.at[0], r_w.at[p], sibling)
        each(0, 3, go)

    @pl.when(jnp.logical_not(carries))
    def _():
        each(0, WINDOW, to_partner)

    @pl.when(carries)
    def _():
        to_partner(0)
    each(0, PARTS, lambda part: along_x(zh, part))
    send(S.at[:, :, 1 - c], Sc, s_st.at[0], r_sc.at[0], sibling)

    k_spread = div(z, 4) * 2 + rem(y, 2)

    def hid_at(k):
        return hid.at[pl.ds(pl.multiple_of(k * 32, 32), 32), :]

    def beside(k4, k):
        send(hid_at(k), hid_at(k), s_h2.at[0], r_h2.at[k], z_to(1))
        send(hid_at(k), hid_at(k), s_h2.at[0], r_h2.at[k], z_to(15))

    @pl.when(is_spread)
    def _():
        each(0, 8, lambda i: done(hx.at[i], r_h1.at[i]))
        r, s = iota((128, 128), 0), iota((128, 128), 1)
        perm = ((s >> 4) == (r & 7)) & (((s >> 2) & 3) == (r >> 5)) & ((s & 3) == ((r >> 3) & 3))
        rows = jnp.dot(
            jnp.where(perm, 1.0, 0.0).astype(BF16), hx[...].reshape(128, 512), preferred_element_type=F32
        ).astype(BF16)
        for q in range(4):
            hid[pl.ds(pl.multiple_of(k_spread * 32, 32), 32), pl.ds(q * 512, 512)] = rows[q * 32:(q + 1) * 32]
        for i, d in enumerate((4, 12, 8)):
            send(hid_at(k_spread), hid_at(k_spread), s_h2.at[0], r_h2.at[k_spread], z_to(d))
        beside(div(z, 4), k_spread)

    done(Sc, r_sc.at[0])
    for h in range(2):
        for x_ in range(4):
            A[x_, h] = S[h, x_, c] + Sc[h, x_]

    each(0, PARTS, lambda part: from_x(zh, part))
    each(1, 4, lambda d: send(A.at[rem(x + d, 4)], Sx.at[x], s_st.at[1], r_sx.at[x], x_to(d)))

    place = rem(z + 16 - x, 4)

    @pl.when(carries)
    def _():
        def go(i):
            k4 = rem(div(z + 17 - x, 4) + i + div(i, 2) * (1 - 2 * rem(i, 2)), 4)
            k = k4 * 2 + rem(y, 2)
            own = jnp.logical_and(is_spread, k == k_spread)

            @pl.when(jnp.logical_not(own))
            def _():
                done(hid_at(k), r_h2.at[k])

            @pl.when(jnp.logical_and(is_spread, k != k_spread))
            def _():
                beside(k4, k)

            @pl.when(jnp.logical_and(place == 1, rem(k4, 2) == 0))
            def _():
                send(hid_at(k), hid_at(k), s_h2.at[0], r_h2.at[k], z_to(1))

            @pl.when(jnp.logical_and(place == 3, rem(k4, 2) == 1))
            def _():
                send(hid_at(k), hid_at(k), s_h2.at[0], r_h2.at[k], z_to(15))

            each(1, 4, lambda d: send(hid_at(k), hid_at(k), s_h3.at[0], r_h2.at[k], y_to(d)))
        each(0, 4, go)
        to_partner(1)

    each(1, 4, lambda d: done(Sx.at[rem(x + d, 4)], r_sx.at[rem(x + d, 4)]))
    total = A[x] + Sx[rem(x + 1, 4)] + Sx[rem(x + 2, 4)] + Sx[rem(x + 3, 4)]
    T[0] = total[:, :, :1024]
    T[1] = total[:, :, 1024:]

    for part in range(PARTS):
        p = piece(1 - zh, x, c, part)
        done(w_at(p), r_w.at[p])
        if part + WINDOW < PARTS:
            to_partner(part + WINDOW)
        along_x(1 - zh, part)
        if part > 0:
            from_x(1 - zh, part - 1)
    send(T.at[1 - zh], Sz, s_st.at[4], r_sz.at[0], partner)
    send(lab.at[zh], lab.at[zh], s_st.at[5], r_lab.at[0], partner)
    def from_sibling(zg):
        def go(i):
            p = (zg * 8 + div(i, PARTS) * 2 + 1 - c) * PARTS + rem(i, PARTS)
            done(w_at(p), r_w.at[p])
        each(0, 4 * PARTS, go)

    def scores(zg, add):
        depth = pl.ds(pl.multiple_of(zg * 1024, 1024), 1024)

        def go(n):
            cols = pl.ds(pl.multiple_of(n * 256, 256), 256)
            part = jnp.dot(hid[:, depth], W[depth, cols], preferred_element_type=F32)
            L[:, cols] = L[:, cols] + part if add else part
        each(0, 4, go)

    from_x(1 - zh, PARTS - 1)
    def last_hidden(k):
        @pl.when(jnp.logical_not(jnp.logical_and(carries, rem(y, 2) == rem(k, 2))))
        def _():
            done(hid_at(k), r_h2.at[k])
    each(0, 8, last_hidden)
    from_sibling(zh)
    scores(zh, False)

    from_sibling(1 - zh)
    scores(1 - zh, True)

    def local_stats(n):
        rows = pl.ds(pl.multiple_of(n * 32, 32), 32)
        logits = L[rows, :]
        top = jnp.max(logits, axis=1, keepdims=True)
        low = logits - top
        e = jnp.exp(low)
        Eb[rows, :] = e.astype(BF16)
        Cb[rows, :] = low.astype(BF16)
        mbuf[rows, :] = jnp.broadcast_to(top, (32, 128))
        sbuf[rows, :] = jnp.broadcast_to(jnp.sum(e, axis=1, keepdims=True), (32, 128))
    each(0, 8, local_stats)

    cross = fold_tokens(lax.dot_general(
        Eb[...], Cb[...], (((1,), (1,)), ((), ())), preferred_element_type=F32))
    tops = mbuf[...]
    tops = fold_tokens(jnp.concatenate([tops, tops], axis=1))
    sums = sbuf[...]
    sums = fold_tokens(jnp.concatenate([sums, sums], axis=1))
    local_top = own_lane(tops)
    cross = cross + sums * local_top
    yb[y, 0:2] = cross.reshape(2, 8, 256)
    yb[y, 2:4] = jnp.concatenate([tops[:, :128], sums[:, 128:]], axis=1).reshape(2, 8, 256)
    each(1, 4, lambda d: send(yb.at[y], yb.at[y], s_y.at[0], r_y.at[y], y_to(d)))

    done(Sz, r_sz.at[0])
    student = (T[zh] + Sz[...]).reshape(16, 1024)
    SL[...] = student
    s_top = jnp.max(student, axis=1, keepdims=True)
    s_sum = jnp.sum(jnp.exp(student - s_top), axis=1, keepdims=True)
    mine_tok = row_token(iota((16, 128), 1)) == iota((16, 128), 0)
    s_top = jnp.sum(jnp.where(mine_tok, s_top, 0.0), axis=0, keepdims=True)
    s_sum = jnp.sum(jnp.where(mine_tok, s_sum, 0.0), axis=0, keepdims=True)
    ys[pl.ds(y, 1)] = jnp.concatenate([s_top, s_sum], axis=0)[None]
    each(1, 4, lambda d: send(ys.at[y], ys.at[y], s_ys.at[0], r_ys.at[y], y_to(d)))

    each(1, 4, lambda d: done(yb.at[rem(y + d, 4)], r_y.at[rem(y + d, 4)]))
    twice = lambda a: jnp.concatenate([a, a], axis=-1)
    got = yb[...]
    y_top = jnp.max(got[:, 2:4, :, :128], axis=0)
    y_scale = jnp.exp(got[:, 2:4, :, :128] - y_top[None])
    y_sum = jnp.sum(got[:, 2:4, :, 128:] * y_scale, axis=0)
    xb[:, 0, :] = jnp.sum(got[:, 0:2] * twice(y_scale), axis=0).reshape(16, 256)
    xb[:, 1, :] = jnp.concatenate([y_top, y_sum], axis=-1).reshape(16, 256)

    def first_sends_left():
        done(W.at[pl.ds(0, 128), :], s_z.at[0])
        done(W.at[pl.ds(0, 768), :], s_x.at[0])
        done(W.at[pl.ds(0, 1024), :], s_c.at[0])

        @pl.when(jnp.logical_not(is_spread))
        def _():
            done(hx.at[0], s_h1.at[0])

        @pl.when(is_spread)
        def _():
            done(W.at[pl.ds(0, 11 * 64), :], s_h2.at[0])

        @pl.when(jnp.logical_and(carries, rem(place, 2) == 1))
        def _():
            done(W.at[pl.ds(0, 2 * 64), :], s_h2.at[0])

        @pl.when(carries)
        def _():
            done(W.at[pl.ds(0, 12 * 64), :], s_h3.at[0])
        done(Sc, s_st.at[0])
        done(A.at[pl.ds(0, 3)], s_st.at[1])
        done(Sz, s_st.at[4])
        done(lab.at[0], s_st.at[5])
        done(yb.at[pl.ds(0, 3)], s_y.at[0])
        done(ys.at[pl.ds(0, 3)], s_ys.at[0])

    far_first(lambda d: send(xb.at[rem(z + d, 16)], rb.at[z], s_z1.at[0], r_z1.at[0], z_to(d)))
    first_sends_left()
    rb[pl.ds(z, 1)] = xb[pl.ds(z, 1)]
    each(1, 4, lambda d: done(ys.at[rem(y + d, 4)], r_ys.at[rem(y + d, 4)]))
    ytops, ysums = ys[:, 0, :], ys[:, 1, :]
    s_top = jnp.max(ytops, axis=0, keepdims=True)
    s_sum = jnp.sum(ysums * jnp.exp(ytops - s_top), axis=0, keepdims=True)
    done(rb.at[pl.ds(0, 15)], r_z1.at[0])
    z_tops = rb[:, 1, :128]
    z_top = jnp.max(z_tops, axis=0, keepdims=True)
    z_scale = jnp.exp(z_tops - z_top)
    z_sum = jnp.sum(rb[:, 1, 128:] * z_scale, axis=0, keepdims=True)
    z_cross = jnp.sum(rb[:, 0, :] * twice(z_scale), axis=0, keepdims=True) / twice(z_sum)
    lane = iota((1, 256), 1)
    stud = jnp.where((lane & 1) == 0, twice(s_top), twice(s_sum))
    z_norm = jnp.where((lane >> 7) == zh, twice(z_top + jnp.log(z_sum)), stud)
    gb[pl.ds(z, 1)] = jnp.concatenate([z_cross, z_norm], axis=0)[None]
    far_first(lambda d: send(gb.at[z], gb.at[z], s_z2.at[0], r_z2.at[0], z_to(d)))
    done(gb.at[pl.ds(0, 15)], r_z2.at[0])
    norms = gb[:, 1, :]
    norm = own_lane(norms)
    ce = norm - gb[:, 0, :]
    ce_out[...] = ce
    inverse = 1.0 / (1.0 + jnp.sum(ce, axis=0, keepdims=True) / 16.0)
    r, l = iota((256, 256), 0), iota((256, 256), 1)
    by_row = jnp.sum(jnp.where(r == l, inverse, 0.0), axis=1, keepdims=True)
    share = jnp.sum(jnp.where(row_token(r) == row_token(l), by_row, 0.0), axis=0, keepdims=True)
    weights = inverse / share
    agree_out[...] = jnp.broadcast_to(weights * 16.0, (8, 256))
    scale = weights * jnp.exp(local_top - norm)
    spread_w = jnp.where(iota((16, 256), 0) == row_token(iota((16, 256), 1)), scale, 0.0)
    coarse = spread_w.astype(BF16)
    fine = (spread_w - coarse.astype(F32)).astype(BF16)
    soft = jnp.dot(coarse, Eb[...], preferred_element_type=F32) + jnp.dot(fine, Eb[...], preferred_element_type=F32)

    stud = jnp.concatenate([norms[:8, 128:], norms[8:, :128]], axis=0)
    stud_top = jnp.max(stud, axis=0, keepdims=True)
    stud_sums = pltpu.roll(stud, 127, 1)
    even = (iota((16, 128), 1) & 1) == 0
    stud_top = jnp.max(jnp.where(even, stud, -jnp.inf), axis=0, keepdims=True)
    stud_top = jnp.where(even[:1], stud_top, 0.0)
    stud_sum = jnp.sum(jnp.where(even, stud_sums * jnp.exp(jnp.where(even, stud - stud_top, 0.0)), 1.0), axis=0, keepdims=True)
    stud_norm = stud_top + jnp.log(stud_sum)

    done(lab.at[1 - zh], r_lab.at[0])
    lane = iota((16, 128), 1)
    first = (row_token(lane) == iota((16, 128), 0)) & ((lane & 7) == 0)
    s_norm = jnp.sum(jnp.where(first, stud_norm, 0.0), axis=1, keepdims=True)
    ids = lab[...].reshape(16, 128)
    ids = jnp.concatenate([ids] * 8, axis=1)
    onehot = jnp.where(iota((16, 1024), 1) + (v * 2048 + zh * 1024) == ids, HARD_SHARE, 0.0)
    residual = jnp.exp(SL[...] - s_norm) - ((1.0 - HARD_SHARE) * soft + onehot)
    R[zh, xc] = residual.astype(BF16)

    def pass_r(f, xc_, i, to):
        send(R.at[f, xc_], R.at[f, xc_], s_r.at[0], r_r.at[f * 8 + xc_], to)

    def await_r(f, xc_):
        done(R.at[f, xc_], r_r.at[f * 8 + xc_])

    pass_r(zh, xc, 0, partner)
    each(1, 4, lambda d: pass_r(zh, xc, d, x_to(d)))
    pass_r(zh, xc, 4, sibling)

    def relay_r(f, base):
        def go(d):
            xc_ = (rem(x + d, 4)) * 2 + c
            await_r(f, xc_)
            pass_r(f, xc_, base + d, sibling)
        each(1, 4, go)

    relay_r(zh, 4)
    tokens = sh[...].astype(F32).reshape(2, 8, 8, 128)
    tokens = jnp.swapaxes(tokens, 0, 1).reshape(128, 128).astype(BF16)

    def grad(f):
        each(0, 4, lambda i: await_r(f, i * 2 + 1 - c))
        for k in range(2):
            cols = pl.ds(pl.multiple_of(f * 1024 + k * 512, 512), 512)
            grad_out[:, cols] = lax.dot_general(
                tokens, R[f, :, :, pl.ds(k * 512, 512)].reshape(128, 512),
                (((0,), (0,)), ((), ())), preferred_element_type=F32)
    grad(zh)
    await_r(1 - zh, xc)
    each(1, 4, lambda d: pass_r(1 - zh, xc, 7 + d, x_to(d)))
    pass_r(1 - zh, xc, 11, sibling)
    relay_r(1 - zh, 11)
    grad(1 - zh)

    done(xb.at[pl.ds(0, 15)], s_z1.at[0])
    done(gb.at[pl.ds(0, 15)], s_z2.at[0])
    done(W.at[pl.ds(0, 240), :], s_r.at[0])


def on_device(teacher_hidden, teacher_head, student_hidden, student_head, labels):
    hid = teacher_hidden[0].reshape(4, 4, 512).transpose(1, 0, 2).reshape(16, 512)
    lab = jnp.broadcast_to(labels[:, None], (8, 128))
    vmem = lambda shape, dtype=F32: pltpu.VMEM(shape, dtype)
    dma = lambda n: pltpu.SemaphoreType.DMA((n,))
    space = pl.BlockSpec(memory_space=pltpu.VMEM)
    hbm = pl.BlockSpec(memory_space=pl.ANY)
    grad, ce, agree = pl.pallas_call(
        kernel,
        out_shape=(
            jax.ShapeDtypeStruct((128, 2048), F32),
            jax.ShapeDtypeStruct((16, 256), F32),
            jax.ShapeDtypeStruct((8, 256), F32),
        ),
        in_specs=[space, hbm, space, hbm, space],
        out_specs=(space,) * 3,
        scratch_shapes=[
            vmem((128, 2048), BF16), vmem((2048, 1024), BF16), vmem((8, 16, 512), BF16), vmem((256, 2048), BF16),
            vmem((256, 1024)), vmem((256, 1024), BF16), vmem((256, 1024), BF16), vmem((256, 128)), vmem((256, 128)),
            vmem((2, 4, 2, 8, 2048)), vmem((2, 4, 8, 2048)), vmem((4, 2, 8, 2048)), vmem((4, 2, 8, 2048)),
            vmem((2, 2, 8, 1024)), vmem((2, 8, 1024)), vmem((16, 1024)), vmem((2, 8, 128), I32),
            vmem((4, 4, 8, 256)), vmem((4, 2, 128)), vmem((16, 2, 256)), vmem((16, 2, 256)), vmem((16, 2, 256)),
            vmem((2, 8, 16, 1024), BF16),
            dma(1), dma(1), dma(1), dma(1), dma(1), dma(1), dma(6), dma(1), dma(1), dma(1), dma(1), dma(1),
            dma(16 * PARTS), dma(8), dma(8), dma(1), dma(4), dma(1), dma(1), dma(4), dma(4), dma(1), dma(1), dma(16),
            dma(1), dma(1),
        ],
        compiler_params=pltpu.CompilerParams(
            collective_id=0, has_side_effects=True, vmem_limit_bytes=48 << 20
        ),
    )(hid, teacher_head, student_hidden, student_head, lab)
    z_hi = lax.axis_index("teacher") // 8
    ce = lax.dynamic_slice_in_dim(ce.reshape(16, 2, 16, 8), 8 * z_hi, 8, 2)
    agree = lax.dynamic_slice_in_dim(agree[0].reshape(2, 16, 8), 8 * z_hi, 8, 1)
    return (
        ce.transpose(2, 0, 1, 3).reshape(8, 16, 16),
        agree.transpose(1, 0, 2).reshape(8, 16),
        grad,
    )


def solution(mesh):
    return jax.shard_map(
        on_device,
        mesh=mesh,
        in_specs=(
            P("teacher", "vocab", None),
            P("teacher", "vocab"),
            P(None, "teacher"),
            P("teacher", "vocab"),
            P("teacher"),
        ),
        out_specs=(P("teacher", None, None), P("teacher", None), P("teacher", "vocab")),
        check_vma=False,
    )
```

```python
import jax
import jax.numpy as jnp
from jax import lax
from jax.experimental import pallas as pl
from jax.experimental.pallas import tpu as pltpu
from jax.sharding import PartitionSpec as P

HARD_SHARE = 0.3
MESH = pl.DeviceIdType.MESH
F32 = jnp.float32
BF16 = jnp.bfloat16
I32 = jnp.int32
PARTS = 2
ROWS = 128 // PARTS
WINDOW = 2


def iota(shape, dim):
    return lax.broadcasted_iota(I32, shape, dim)


def row_token(r):
    return (r >> 3) & 15


def row_teacher(r):
    return (r >> 7) * 8 + (r & 7)


def fold_tokens(values):
    same = row_token(iota((256, 256), 0)) == row_token(iota((256, 256), 1))
    kept = jnp.where(same, values, 0.0).reshape(2, 16, 8, 256)
    return jnp.sum(kept, axis=1).reshape(16, 256)


def own_lane(values):
    same = iota((16, 256), 0) == row_teacher(iota((16, 256), 1))
    return jnp.sum(jnp.where(same, values, 0.0), axis=0, keepdims=True)


div, rem = lax.div, lax.rem


def kernel(
    hid_in, head, sh, shead_in, lab_in,
    grad_out, ce_out, agree_out,
    shead, W, hx, hid, L, Eb, Cb, mbuf, sbuf,
    S, Sc, A, Sx, T, Sz, SL, lab, yb, ys, xb, rb, gb, R,
    s_z, s_x, s_c, s_h1, s_h2, s_h3, s_st, s_y, s_ys, s_z1, s_z2, s_r,
    r_w, r_h1, r_h2, r_sc, r_sx, r_sz, r_lab, r_y, r_ys, r_z1, r_z2, r_r, l_w, l_in,
):
    t = lax.axis_index("teacher")
    v = lax.axis_index("vocab")
    zh, xc = div(t, 8), rem(t, 8)
    x, c = div(xc, 2), rem(xc, 2)
    zl, y = div(v, 4), rem(v, 4)
    z = zh * 8 + zl

    def dev(z_, xc_, y_):
        return {"teacher": div(z_, 8) * 8 + xc_, "vocab": rem(z_, 8) * 4 + y_}

    def send(src, dst, ssem, rsem, to):
        pltpu.make_async_remote_copy(
            src_ref=src, dst_ref=dst, send_sem=ssem, recv_sem=rsem, device_id=to, device_id_type=MESH
        ).start()

    def done(ref, sem):
        pltpu.make_async_copy(ref, ref, sem).wait()

    def each(lo, hi, body):
        def step(i, carry):
            body(i)
            return carry
        lax.fori_loop(lo, hi, step, 0)

    def far_first(body):
        each(0, 15, lambda i: body(8 + div(i, 2) * (1 - 2 * rem(i, 2)) - rem(i, 2)))

    z_to = lambda d: dev(rem(z + d, 16), xc, y)
    x_to = lambda d: dev(z, rem(x + d, 4) * 2 + c, y)
    y_to = lambda d: dev(z, xc, rem(y + d, 4))
    xc_to = lambda d: dev(z, rem(xc + d, 8), y)
    sibling = dev(z, x * 2 + 1 - c, y)
    partner = z_to(8)

    pltpu.make_async_copy(shead_in, shead, l_in.at[0]).start()
    barrier = pltpu.get_barrier_semaphore()
    each(1, 16, lambda d: pl.semaphore_signal(barrier, inc=1, device_id=z_to(d), device_id_type=MESH))
    each(1, 8, lambda d: pl.semaphore_signal(barrier, inc=1, device_id=xc_to(d), device_id_type=MESH))
    each(1, 4, lambda d: pl.semaphore_signal(barrier, inc=1, device_id=y_to(d), device_id_type=MESH))

    mine = pl.ds(pl.multiple_of(zh * 1024, 1024), 1024)
    other = pl.ds(pl.multiple_of((1 - zh) * 1024, 1024), 1024)
    piece = lambda zh_, x_, c_, part: ((zh_ * 8 + x_ * 2 + c_) * PARTS) + part
    w_at = lambda p: W.at[pl.ds(pl.multiple_of(p * ROWS, ROWS), ROWS), :]
    block = W.at[pl.ds(pl.multiple_of(t * 128, 128), 128), :]
    pltpu.make_async_copy(head.at[:, mine], block, l_w.at[0]).start()
    pltpu.make_async_copy(shead_in, shead, l_in.at[0]).wait()
    for k in range(4):
        cols = pl.ds(k * 512, 512)
        S[:, :, :, :, cols] = jnp.dot(sh[...], shead[:, cols], preferred_element_type=F32).reshape(2, 4, 2, 8, 512)
    lab[pl.ds(zh, 1)] = lab_in[...][None]
    pltpu.make_async_copy(head.at[:, mine], block, l_w.at[0]).wait()
    pl.semaphore_wait(barrier, 25)

    spread = rem(z, 4) * 2 + div(y, 2)
    is_spread = xc == spread
    to_spread = dev(z, spread, y)

    @pl.when(is_spread)
    def _():
        pltpu.make_async_copy(hid_in, hx.at[xc], r_h1.at[xc]).start()

    @pl.when(jnp.logical_not(is_spread))
    def _():
        send(hid_in, hx.at[xc], s_h1.at[0], r_h1.at[xc], to_spread)

    carries = div(y, 2) == c

    def to_partner(part):
        p = piece(zh, x, c, part)
        send(head.at[pl.ds(pl.multiple_of(part * ROWS, ROWS), ROWS), other], w_at(p), s_z.at[0], r_w.at[p], partner)

    def along_x(zg, part):
        p = piece(zg, x, c, part)
        each(1, 4, lambda d: send(w_at(p), w_at(p), s_x.at[0], r_w.at[p], x_to(d)))
        send(w_at(p), w_at(p), s_c.at[0], r_w.at[p], sibling)

    def from_x(zg, part):
        def go(i):
            p = piece(zg, rem(x + 1 + rem(i * 2, 3), 4), c, part)
            done(w_at(p), r_w.at[p])
            send(w_at(p), w_at(p), s_c.at[0], r_w.at[p], sibling)
        each(0, 3, go)

    @pl.when(jnp.logical_not(carries))
    def _():
        each(0, WINDOW, to_partner)

    @pl.when(carries)
    def _():
        to_partner(0)
    each(0, PARTS, lambda part: along_x(zh, part))
    send(S.at[:, :, 1 - c], Sc, s_st.at[0], r_sc.at[0], sibling)

    k_spread = div(z, 4) * 2 + rem(y, 2)

    def hid_at(k):
        return hid.at[pl.ds(pl.multiple_of(k * 32, 32), 32), :]

    def beside(k4, k):
        send(hid_at(k), hid_at(k), s_h2.at[0], r_h2.at[k], z_to(1))
        send(hid_at(k), hid_at(k), s_h2.at[0], r_h2.at[k], z_to(15))

    @pl.when(is_spread)
    def _():
        each(0, 8, lambda i: done(hx.at[i], r_h1.at[i]))
        r, s = iota((128, 128), 0), iota((128, 128), 1)
        perm = ((s >> 4) == (r & 7)) & (((s >> 2) & 3) == (r >> 5)) & ((s & 3) == ((r >> 3) & 3))
        rows = jnp.dot(
            jnp.where(perm, 1.0, 0.0).astype(BF16), hx[...].reshape(128, 512), preferred_element_type=F32
        ).astype(BF16)
        for q in range(4):
            hid[pl.ds(pl.multiple_of(k_spread * 32, 32), 32), pl.ds(q * 512, 512)] = rows[q * 32:(q + 1) * 32]
        for i, d in enumerate((4, 12, 8)):
            send(hid_at(k_spread), hid_at(k_spread), s_h2.at[0], r_h2.at[k_spread], z_to(d))
        beside(div(z, 4), k_spread)

    done(Sc, r_sc.at[0])
    for h in range(2):
        for x_ in range(4):
            A[x_, h] = S[h, x_, c] + Sc[h, x_]

    each(0, PARTS, lambda part: from_x(zh, part))
    each(1, 4, lambda d: send(A.at[rem(x + d, 4)], Sx.at[x], s_st.at[1], r_sx.at[x], x_to(d)))

    place = rem(z + 16 - x, 4)

    @pl.when(carries)
    def _():
        def go(i):
            k4 = rem(div(z + 17 - x, 4) + i + div(i, 2) * (1 - 2 * rem(i, 2)), 4)
            k = k4 * 2 + rem(y, 2)
            own = jnp.logical_and(is_spread, k == k_spread)

            @pl.when(jnp.logical_not(own))
            def _():
                done(hid_at(k), r_h2.at[k])

            @pl.when(jnp.logical_and(is_spread, k != k_spread))
            def _():
                beside(k4, k)

            @pl.when(jnp.logical_and(place == 1, rem(k4, 2) == 0))
            def _():
                send(hid_at(k), hid_at(k), s_h2.at[0], r_h2.at[k], z_to(1))

            @pl.when(jnp.logical_and(place == 3, rem(k4, 2) == 1))
            def _():
                send(hid_at(k), hid_at(k), s_h2.at[0], r_h2.at[k], z_to(15))

            each(1, 4, lambda d: send(hid_at(k), hid_at(k), s_h3.at[0], r_h2.at[k], y_to(d)))
        each(0, 4, go)
        to_partner(1)

    each(1, 4, lambda d: done(Sx.at[rem(x + d, 4)], r_sx.at[rem(x + d, 4)]))
    total = A[x] + Sx[rem(x + 1, 4)] + Sx[rem(x + 2, 4)] + Sx[rem(x + 3, 4)]
    T[0] = total[:, :, :1024]
    T[1] = total[:, :, 1024:]

    for part in range(PARTS):
        p = piece(1 - zh, x, c, part)
        done(w_at(p), r_w.at[p])
        if part + WINDOW < PARTS:
            to_partner(part + WINDOW)
        along_x(1 - zh, part)
        if part > 0:
            from_x(1 - zh, part - 1)
    send(T.at[1 - zh], Sz, s_st.at[4], r_sz.at[0], partner)
    send(lab.at[zh], lab.at[zh], s_st.at[5], r_lab.at[0], partner)
    def from_sibling(zg):
        def go(i):
            p = (zg * 8 + div(i, PARTS) * 2 + 1 - c) * PARTS + rem(i, PARTS)
            done(w_at(p), r_w.at[p])
        each(0, 4 * PARTS, go)

    def scores(zg, add):
        depth = pl.ds(pl.multiple_of(zg * 1024, 1024), 1024)

        def go(n):
            cols = pl.ds(pl.multiple_of(n * 256, 256), 256)
            part = jnp.dot(hid[:, depth], W[depth, cols], preferred_element_type=F32)
            L[:, cols] = L[:, cols] + part if add else part
        each(0, 4, go)

    from_x(1 - zh, PARTS - 1)
    def last_hidden(k):
        @pl.when(jnp.logical_not(jnp.logical_and(carries, rem(y, 2) == rem(k, 2))))
        def _():
            done(hid_at(k), r_h2.at[k])
    each(0, 8, last_hidden)
    from_sibling(zh)
    scores(zh, False)

    from_sibling(1 - zh)
    scores(1 - zh, True)

    def local_stats(n):
        rows = pl.ds(pl.multiple_of(n * 32, 32), 32)
        logits = L[rows, :]
        top = jnp.max(logits, axis=1, keepdims=True)
        low = logits - top
        e = jnp.exp(low)
        Eb[rows, :] = e.astype(BF16)
        Cb[rows, :] = low.astype(BF16)
        mbuf[rows, :] = jnp.broadcast_to(top, (32, 128))
        sbuf[rows, :] = jnp.broadcast_to(jnp.sum(e, axis=1, keepdims=True), (32, 128))
    each(0, 8, local_stats)

    cross = fold_tokens(lax.dot_general(
        Eb[...], Cb[...], (((1,), (1,)), ((), ())), preferred_element_type=F32))
    tops = mbuf[...]
    tops = fold_tokens(jnp.concatenate([tops, tops], axis=1))
    sums = sbuf[...]
    sums = fold_tokens(jnp.concatenate([sums, sums], axis=1))
    local_top = own_lane(tops)
    cross = cross + sums * local_top
    yb[y, 0:2] = cross.reshape(2, 8, 256)
    yb[y, 2:4] = jnp.concatenate([tops[:, :128], sums[:, 128:]], axis=1).reshape(2, 8, 256)
    each(1, 4, lambda d: send(yb.at[y], yb.at[y], s_y.at[0], r_y.at[y], y_to(d)))

    each(1, 4, lambda d: done(yb.at[rem(y + d, 4)], r_y.at[rem(y + d, 4)]))
    twice = lambda a: jnp.concatenate([a, a], axis=-1)
    got = yb[...]
    y_top = jnp.max(got[:, 2:4, :, :128], axis=0)
    y_scale = jnp.exp(got[:, 2:4, :, :128] - y_top[None])
    y_sum = jnp.sum(got[:, 2:4, :, 128:] * y_scale, axis=0)
    xb[:, 0, :] = jnp.sum(got[:, 0:2] * twice(y_scale), axis=0).reshape(16, 256)
    xb[:, 1, :] = jnp.concatenate([y_top, y_sum], axis=-1).reshape(16, 256)

    def first_sends_left():
        done(W.at[pl.ds(0, 128), :], s_z.at[0])
        done(W.at[pl.ds(0, 768), :], s_x.at[0])
        done(W.at[pl.ds(0, 1024), :], s_c.at[0])

        @pl.when(jnp.logical_not(is_spread))
        def _():
            done(hx.at[0], s_h1.at[0])

        @pl.when(is_spread)
        def _():
            done(W.at[pl.ds(0, 11 * 64), :], s_h2.at[0])

        @pl.when(jnp.logical_and(carries, rem(place, 2) == 1))
        def _():
            done(W.at[pl.ds(0, 2 * 64), :], s_h2.at[0])

        @pl.when(carries)
        def _():
            done(W.at[pl.ds(0, 12 * 64), :], s_h3.at[0])
        done(Sc, s_st.at[0])
        done(A.at[pl.ds(0, 3)], s_st.at[1])
        done(Sz, s_st.at[4])
        done(lab.at[0], s_st.at[5])
        done(yb.at[pl.ds(0, 3)], s_y.at[0])
        done(ys.at[pl.ds(0, 3)], s_ys.at[0])

    far_first(lambda d: send(xb.at[rem(z + d, 16)], rb.at[z], s_z1.at[0], r_z1.at[0], z_to(d)))

    done(Sz, r_sz.at[0])
    student = (T[zh] + Sz[...]).reshape(16, 1024)
    SL[...] = student
    s_top = jnp.max(student, axis=1, keepdims=True)
    s_sum = jnp.sum(jnp.exp(student - s_top), axis=1, keepdims=True)
    mine_tok = row_token(iota((16, 128), 1)) == iota((16, 128), 0)
    s_top = jnp.sum(jnp.where(mine_tok, s_top, 0.0), axis=0, keepdims=True)
    s_sum = jnp.sum(jnp.where(mine_tok, s_sum, 0.0), axis=0, keepdims=True)
    ys[pl.ds(y, 1)] = jnp.concatenate([s_top, s_sum], axis=0)[None]
    each(1, 4, lambda d: send(ys.at[y], ys.at[y], s_ys.at[0], r_ys.at[y], y_to(d)))

    rb[pl.ds(z, 1)] = xb[pl.ds(z, 1)]
    each(1, 4, lambda d: done(ys.at[rem(y + d, 4)], r_ys.at[rem(y + d, 4)]))
    ytops, ysums = ys[:, 0, :], ys[:, 1, :]
    s_top = jnp.max(ytops, axis=0, keepdims=True)
    s_sum = jnp.sum(ysums * jnp.exp(ytops - s_top), axis=0, keepdims=True)
    done(rb.at[pl.ds(0, 15)], r_z1.at[0])
    z_tops = rb[:, 1, :128]
    z_top = jnp.max(z_tops, axis=0, keepdims=True)
    z_scale = jnp.exp(z_tops - z_top)
    z_sum = jnp.sum(rb[:, 1, 128:] * z_scale, axis=0, keepdims=True)
    z_cross = jnp.sum(rb[:, 0, :] * twice(z_scale), axis=0, keepdims=True) / twice(z_sum)
    lane = iota((1, 256), 1)
    stud = jnp.where((lane & 1) == 0, twice(s_top), twice(s_sum))
    z_norm = jnp.where((lane >> 7) == zh, twice(z_top + jnp.log(z_sum)), stud)
    gb[pl.ds(z, 1)] = jnp.concatenate([z_cross, z_norm], axis=0)[None]
    far_first(lambda d: send(gb.at[z], gb.at[z], s_z2.at[0], r_z2.at[0], z_to(d)))
    done(gb.at[pl.ds(0, 15)], r_z2.at[0])
    norms = gb[:, 1, :]
    norm = own_lane(norms)
    ce = norm - gb[:, 0, :]
    ce_out[...] = ce
    inverse = 1.0 / (1.0 + jnp.sum(ce, axis=0, keepdims=True) / 16.0)
    r, l = iota((256, 256), 0), iota((256, 256), 1)
    by_row = jnp.sum(jnp.where(r == l, inverse, 0.0), axis=1, keepdims=True)
    share = jnp.sum(jnp.where(row_token(r) == row_token(l), by_row, 0.0), axis=0, keepdims=True)
    weights = inverse / share
    agree_out[...] = jnp.broadcast_to(weights * 16.0, (8, 256))
    scale = weights * jnp.exp(local_top - norm)
    spread_w = jnp.where(iota((16, 256), 0) == row_token(iota((16, 256), 1)), scale, 0.0)
    coarse = spread_w.astype(BF16)
    fine = (spread_w - coarse.astype(F32)).astype(BF16)
    soft = jnp.dot(coarse, Eb[...], preferred_element_type=F32) + jnp.dot(fine, Eb[...], preferred_element_type=F32)

    stud = jnp.concatenate([norms[:8, 128:], norms[8:, :128]], axis=0)
    stud_top = jnp.max(stud, axis=0, keepdims=True)
    stud_sums = pltpu.roll(stud, 127, 1)
    even = (iota((16, 128), 1) & 1) == 0
    stud_top = jnp.max(jnp.where(even, stud, -jnp.inf), axis=0, keepdims=True)
    stud_top = jnp.where(even[:1], stud_top, 0.0)
    stud_sum = jnp.sum(jnp.where(even, stud_sums * jnp.exp(jnp.where(even, stud - stud_top, 0.0)), 1.0), axis=0, keepdims=True)
    stud_norm = stud_top + jnp.log(stud_sum)

    done(lab.at[1 - zh], r_lab.at[0])
    lane = iota((16, 128), 1)
    first = (row_token(lane) == iota((16, 128), 0)) & ((lane & 7) == 0)
    s_norm = jnp.sum(jnp.where(first, stud_norm, 0.0), axis=1, keepdims=True)
    ids = lab[...].reshape(16, 128)
    ids = jnp.concatenate([ids] * 8, axis=1)
    onehot = jnp.where(iota((16, 1024), 1) + (v * 2048 + zh * 1024) == ids, HARD_SHARE, 0.0)
    residual = jnp.exp(SL[...] - s_norm) - ((1.0 - HARD_SHARE) * soft + onehot)
    R[zh, xc] = residual.astype(BF16)

    def pass_r(f, xc_, i, to):
        send(R.at[f, xc_], R.at[f, xc_], s_r.at[0], r_r.at[f * 8 + xc_], to)

    def await_r(f, xc_):
        done(R.at[f, xc_], r_r.at[f * 8 + xc_])

    pass_r(zh, xc, 0, partner)
    each(1, 4, lambda d: pass_r(zh, xc, d, x_to(d)))
    pass_r(zh, xc, 4, sibling)

    def relay_r(f, base):
        def go(d):
            xc_ = (rem(x + d, 4)) * 2 + c
            await_r(f, xc_)
            pass_r(f, xc_, base + d, sibling)
        each(1, 4, go)

    relay_r(zh, 4)
    tokens = sh[...].astype(F32).reshape(2, 8, 8, 128)
    tokens = jnp.swapaxes(tokens, 0, 1).reshape(128, 128).astype(BF16)

    def grad(f):
        each(0, 4, lambda i: await_r(f, i * 2 + 1 - c))
        for k in range(2):
            cols = pl.ds(pl.multiple_of(f * 1024 + k * 512, 512), 512)
            grad_out[:, cols] = lax.dot_general(
                tokens, R[f, :, :, pl.ds(k * 512, 512)].reshape(128, 512),
                (((0,), (0,)), ((), ())), preferred_element_type=F32)
    grad(zh)
    await_r(1 - zh, xc)
    each(1, 4, lambda d: pass_r(1 - zh, xc, 7 + d, x_to(d)))
    pass_r(1 - zh, xc, 11, sibling)
    relay_r(1 - zh, 11)
    grad(1 - zh)

    first_sends_left()
    done(xb.at[pl.ds(0, 15)], s_z1.at[0])
    done(gb.at[pl.ds(0, 15)], s_z2.at[0])
    done(W.at[pl.ds(0, 240), :], s_r.at[0])


def on_device(teacher_hidden, teacher_head, student_hidden, student_head, labels):
    hid = teacher_hidden[0].reshape(4, 4, 512).transpose(1, 0, 2).reshape(16, 512)
    lab = jnp.broadcast_to(labels[:, None], (8, 128))
    vmem = lambda shape, dtype=F32: pltpu.VMEM(shape, dtype)
    dma = lambda n: pltpu.SemaphoreType.DMA((n,))
    space = pl.BlockSpec(memory_space=pltpu.VMEM)
    hbm = pl.BlockSpec(memory_space=pl.ANY)
    grad, ce, agree = pl.pallas_call(
        kernel,
        out_shape=(
            jax.ShapeDtypeStruct((128, 2048), F32),
            jax.ShapeDtypeStruct((16, 256), F32),
            jax.ShapeDtypeStruct((8, 256), F32),
        ),
        in_specs=[space, hbm, space, hbm, space],
        out_specs=(space,) * 3,
        scratch_shapes=[
            vmem((128, 2048), BF16), vmem((2048, 1024), BF16), vmem((8, 16, 512), BF16), vmem((256, 2048), BF16),
            vmem((256, 1024)), vmem((256, 1024), BF16), vmem((256, 1024), BF16), vmem((256, 128)), vmem((256, 128)),
            vmem((2, 4, 2, 8, 2048)), vmem((2, 4, 8, 2048)), vmem((4, 2, 8, 2048)), vmem((4, 2, 8, 2048)),
            vmem((2, 2, 8, 1024)), vmem((2, 8, 1024)), vmem((16, 1024)), vmem((2, 8, 128), I32),
            vmem((4, 4, 8, 256)), vmem((4, 2, 128)), vmem((16, 2, 256)), vmem((16, 2, 256)), vmem((16, 2, 256)),
            vmem((2, 8, 16, 1024), BF16),
            dma(1), dma(1), dma(1), dma(1), dma(1), dma(1), dma(6), dma(1), dma(1), dma(1), dma(1), dma(1),
            dma(16 * PARTS), dma(8), dma(8), dma(1), dma(4), dma(1), dma(1), dma(4), dma(4), dma(1), dma(1), dma(16),
            dma(1), dma(1),
        ],
        compiler_params=pltpu.CompilerParams(
            collective_id=0, has_side_effects=True, vmem_limit_bytes=48 << 20
        ),
    )(hid, teacher_head, student_hidden, student_head, lab)
    z_hi = lax.axis_index("teacher") // 8
    ce = lax.dynamic_slice_in_dim(ce.reshape(16, 2, 16, 8), 8 * z_hi, 8, 2)
    agree = lax.dynamic_slice_in_dim(agree[0].reshape(2, 16, 8), 8 * z_hi, 8, 1)
    return (
        ce.transpose(2, 0, 1, 3).reshape(8, 16, 16),
        agree.transpose(1, 0, 2).reshape(8, 16),
        grad,
    )


def solution(mesh):
    return jax.shard_map(
        on_device,
        mesh=mesh,
        in_specs=(
            P("teacher", "vocab", None),
            P("teacher", "vocab"),
            P(None, "teacher"),
            P("teacher", "vocab"),
            P("teacher"),
        ),
        out_specs=(P("teacher", None, None), P("teacher", None), P("teacher", "vocab")),
        check_vma=False,
    )
```
